512 devices in a mesh: dp: 32 (over x, y), tensor: 16 (over z, core).
Axes of the slice: x: 4, y: 8, z: 8, core: 2. Of those that a mesh axis runs over, the one named last changes fastest.
Arguments:
- features: bfloat16 [16384, 1280], P('dp'), may hold values from -6 to 6
- class_bias: float32 [12288], P('tensor')
- logits: bfloat16 [16384, 12288], P('dp', 'tensor'), may hold values from -12 to 12
- tile_lists: int32 [512, 2], P('dp'), may hold values from 0 to 31, all different within a row; in each aligned block of 16 rows (0 to 15, 16 to 31, ...) at most 2 rows name the same one
- valid_counts: int32 [32], P('dp'), may hold values from 192 to 512, as said below
Outputs:
- log_labels: float32 [16384, 12288], P('dp', 'tensor')
The draws below stay inside these ranges and needn't reach their ends.
Inputs may be any that keep to these rules, and one draw needn't show every extreme that they name: `tile_lists`: each row names 2 different tiles; among the 16 rows of one index of dp no tile is named more than 2 times. `valid_counts`: some tile is fully valid.
All inputs are finite; a program needn't handle non-finite values.
Results may differ from the reference program's by a relative error of at most 0.0005.
Values may be sent and summed in bfloat16 or wider, within the bound.
No kernel may reach another device: no remote copies, remote signals or barrier semaphores. Data moves between devices by JAX's collectives and lax.ppermute only.
A program may use at most 128 MiB of HBM per device.

```python
import math
import jax
import jax.numpy as jnp
import numpy as np
from jax import lax

D = 1280
TILE = 512
QB = 32
NT = 2
SWEEPS = 2
NBLK = 16
CAP = 2
TILES = 32
ROWS = 16384
BLOCKS = 512
CLS = 12288


def draw_class_bias(key, part):
    index = jnp.arange(CLS, dtype=jnp.float32)
    noise = jnp.clip(jax.random.normal(key, (CLS,), jnp.float32), -2.5, 2.5)
    return 1.2 * index / CLS + 0.5 * noise


def draw_valid_counts(key, part):
    first_key = jax.random.fold_in(key, 11)
    second_key = jax.random.fold_in(key, 23)
    member_counts = jax.random.randint(first_key, (TILES,), 3 * TILE // 8, TILE + 1)
    where_full = jax.random.randint(second_key, (), 0, TILES)
    return member_counts.at[where_full].set(TILE)


def levels(key, dims, cuts, least, top_value):
    gain = 1.0
    for position, shards_of in cuts:
        heights = jax.random.uniform(jax.random.fold_in(jax.random.fold_in(key, 6), position), (shards_of,), jnp.float32, least / len(cuts), top_value / len(cuts))
        gain = gain * jnp.repeat(jnp.exp(heights), dims[position] // shards_of).reshape((-1,) + (1,) * (len(dims) - 1 - position))
    return gain


def deal_out(key, own, number, rows, count, top, bound, slope):
    sequence = jax.random.permutation(key, count)
    packed, ordinary = load_shares(count, rows * top, bound, slope, True), load_shares(count, rows * top, bound, slope, False)
    places = jnp.arange(count)

    def named(sizes, offset_by):
        used = int((sizes > 0).sum())
        fixed = max(1, used // 4)
        moved = fixed + (places - fixed + offset_by * (used - fixed)) % max(1, count - fixed)
        return jnp.zeros((count,), jnp.int32).at[sequence[jnp.where(places < fixed, places, moved)]].set(jnp.asarray(sizes, jnp.int32))

    sizes = jnp.where(number % 4 == 0, named(packed, number // 4), named(ordinary, number - number // 4 - 1))
    mixed = jax.random.permutation(jax.random.fold_in(own, 3), count)
    source_of, taker = mixed[0:count // 2 * 2:2], mixed[1:count // 2 * 2:2]
    room = jnp.minimum(sizes[source_of] - 1, bound - sizes[taker]) // 2
    room = jnp.where((source_of == sequence[0]) | (taker == sequence[0]) | (sizes[taker] == 0), 0, jnp.maximum(room, 0))
    moved = jax.random.randint(jax.random.fold_in(own, 4), (count // 2,), 0, 1 << 20) % (room + 1)
    sizes = sizes.at[source_of].add(-moved).at[taker].add(moved)
    items = jnp.searchsorted(jnp.cumsum(sizes), jnp.arange(rows * top), side="right").astype(jnp.int32)
    listing = items.reshape(top, rows).T
    listing = listing[jax.random.permutation(jax.random.fold_in(own, 1), rows)]
    offset_by = jax.random.randint(jax.random.fold_in(own, 2), (rows, 1), 0, top)
    return jnp.take_along_axis(listing, (jnp.arange(top)[None, :] + offset_by) % top, axis=1)


def load_shares(amount, total, limit, lean, full):
    portions = [(1 << 20) // math.isqrt(rank ** lean) + 1 for rank in range(1, amount + 1)]
    largest = limit if full else min(limit, max(-(-total // amount), total * portions[0] // sum(portions)))
    least = 1 if total - largest >= amount - 1 else 0
    given, rest = [largest] + [least] * (amount - 1), total - largest - least * (amount - 1)
    while rest > 0:
        movable = [i for i in range(1, amount) if given[i] < largest] or [i for i in range(1, amount) if given[i] < limit]
        whole, budget = sum([portions[i] for i in movable]), rest
        for i in movable:
            more = min(limit - given[i], max(1, budget * portions[i] // whole), rest)
            given[i] = given[i] + more
            rest = rest - more
    return np.array(given)


def centred(stream_key, shape, scale, bound, pieces=(), held_as=jnp.bfloat16):
    drawn = jax.random.normal(stream_key, shape, jnp.float32) * scale
    if len(pieces) > 0:
        drawn = levels(stream_key, shape, pieces, -0.22, 0.18) * drawn
    return jnp.clip(drawn, min=-bound, max=bound).astype(held_as)


def setup_inputs(seed: int = 0) -> dict:
    keys = jax.random.split(jax.random.key(seed), 6)
    features = centred(keys[0], (ROWS, D), 1.0, 6.0, ((0, 32),))
    class_bias = draw_class_bias(jax.random.fold_in(keys[5], 71), 0)
    logits = centred(keys[2], (ROWS, CLS), 3.0, 12.0, ((0, 32), (1, 16)))
    tile_lists_keys = jax.random.split(jax.random.fold_in(keys[3], 1), BLOCKS // NBLK)
    tile_lists_turns = jax.random.permutation(jax.random.fold_in(keys[3], 3), BLOCKS // NBLK)
    tile_lists = jax.vmap(lambda own, number: deal_out(jax.random.fold_in(keys[3], 2), own, number, NBLK, TILES, NT, CAP, 2))(tile_lists_keys, tile_lists_turns).reshape((BLOCKS, NT))
    valid_counts = draw_valid_counts(jax.random.fold_in(keys[5], 71), 0)
    return dict(features=features, class_bias=class_bias, logits=logits, tile_lists=tile_lists, valid_counts=valid_counts)


ALPHA = 0.75
SOFTMAX_TEMPER = 0.05
EPSILON = 1e-06

def unitnorm_rows(features):
    wide = features.astype(jnp.float32)
    scale = lax.rsqrt(lax.optimization_barrier(jnp.mean(wide * wide, axis=1, keepdims=True)) + EPSILON)
    return (wide * scale / math.sqrt(wide.shape[1])).astype(jnp.bfloat16)

def reference(features, class_bias, logits, tile_lists, valid_counts):
    adjusted = logits.astype(jnp.float32) + class_bias[None, :]
    exponentials = jnp.exp(adjusted)
    prior = (exponentials / lax.optimization_barrier(jnp.sum(exponentials, axis=1))[:, None]).astype(jnp.bfloat16)
    normalized = unitnorm_rows(features)
    query_blocks = normalized.reshape(BLOCKS, QB, D)
    columns = jnp.arange(TILE, dtype=jnp.int32)

    def block_weights(inputs):
        query_vectors, tile_ids = inputs

        def one_tile(tile_number):
            tile_row_block = lax.dynamic_slice_in_dim(normalized, (tile_number * TILE).astype(jnp.int32), TILE, 0)
            affinity_scores = jnp.dot(query_vectors, tile_row_block.T, preferred_element_type=jnp.float32) / SOFTMAX_TEMPER
            return jnp.where(columns[None, :] < valid_counts[tile_number], jnp.exp(affinity_scores), 0.0).astype(jnp.bfloat16)
        return jax.vmap(one_tile)(tile_ids)
    weights = lax.map(block_weights, (query_blocks, tile_lists))
    denominator = lax.optimization_barrier(jnp.sum(lax.optimization_barrier(jnp.sum(weights.astype(jnp.float32), axis=3)), axis=1)).reshape(ROWS)
    prior_float = prior.astype(jnp.float32)
    label_matrix = prior
    spread = prior_float
    for sweep_index in range(SWEEPS):
        current = label_matrix

        def block_numerator(inputs):
            block_weight, tile_ids = inputs

            def one_tile(tile_weight, tile_number):
                tile_row_block = lax.dynamic_slice_in_dim(current, (tile_number * TILE).astype(jnp.int32), TILE, 0)
                partial_sum = jnp.dot(tile_weight, tile_row_block, preferred_element_type=jnp.float32).astype(jnp.bfloat16)
                return lax.optimization_barrier(partial_sum).astype(jnp.float32)
            return lax.optimization_barrier(jnp.sum(jax.vmap(one_tile)(block_weight, tile_ids), axis=0))
        numerator = lax.map(block_numerator, (weights, tile_lists)).reshape(ROWS, CLS)
        spread = ALPHA * numerator / denominator[:, None] + (1.0 - ALPHA) * prior_float
        label_matrix = spread.astype(jnp.bfloat16)
    return jnp.log(spread)
```

```python
import math

import jax
import jax.numpy as jnp
from jax import lax
from jax.experimental import pallas as pl
from jax.experimental.pallas import tpu as pltpu
from jax.sharding import Mesh
from jax.sharding import PartitionSpec as P

ALPHA = 0.75
SOFTMAX_TEMPER = 0.05
EPSILON = 1e-06

NX, NY, NZ, NC = 4, 8, 8, 2
TILES = NX * NY
TILE = 512
QB = 32
NBLK = 16
NT = 2
PER = NBLK * NT
SLOTS = TILES * 2
SUB = 2
ROWS_C = QB // NC
BF = jnp.bfloat16
F32 = jnp.float32


def unitnorm_rows(features):
    wide = features.astype(F32)
    scale = lax.rsqrt(jnp.mean(wide * wide, axis=-1, keepdims=True) + EPSILON)
    return (wide * scale / math.sqrt(wide.shape[-1])).astype(BF)


def sweep_kernel(index_ref, w_ref, prior_ref, own, after, oppa, oppb, before, out_ref, held, sems):
    y = pl.program_id(0)

    @pl.when(y == 0)
    def _():
        half = NY // 2
        places = (
            (own, 0, NY),
            (after, NY, NY),
            (oppa, 2 * NY, half),
            (oppb, 2 * NY + half, half),
            (before, 3 * NY, NY),
        )
        copies = [
            pltpu.make_async_copy(src, held.at[pl.ds(at, n)], sems.at[i])
            for i, (src, at, n) in enumerate(places)
        ]
        for copy in copies:
            copy.start()
        for copy in copies:
            copy.wait()

    classes = out_ref.shape[1]
    lanes = lax.broadcasted_iota(jnp.int32, (classes, 128), 1) // QB
    for group in range(NBLK // 4):
        total = None
        for k in range(NT):
            weights = jnp.concatenate(
                [
                    w_ref[c, pl.ds((4 * group + b) * ROWS_C, ROWS_C), pl.ds(k * TILE, TILE)]
                    for b in range(4)
                    for c in range(NC)
                ],
                axis=0,
            )
            labels = jnp.concatenate(
                [held[index_ref[y * PER + (4 * group + b) * NT + k]] for b in range(4)], axis=0
            )
            sums = lax.dot_general(
                labels, weights, (((1,), (1,)), ((), ())), preferred_element_type=F32
            )
            total = sums if total is None else total + sums
        picked = total[:classes]
        for b in range(1, 4):
            picked = jnp.where(lanes == b, total[b * classes : (b + 1) * classes], picked)
        at = pl.ds(128 * group, 128)
        prior = prior_ref[0, :, at].astype(F32)
        out_ref[0, :, at] = (picked + (1.0 - ALPHA) * prior).astype(BF)


def sweep(index, weights, prior, pieces):
    ny, classes, rows = prior.shape
    return pl.pallas_call(
        sweep_kernel,
        grid_spec=pltpu.PrefetchScalarGridSpec(
            num_scalar_prefetch=1,
            grid=(ny,),
            in_specs=[
                pl.BlockSpec((NC,) + weights.shape[1:], lambda y, _: (y, 0, 0)),
                pl.BlockSpec((1, classes, rows), lambda y, _: (y, 0, 0)),
            ]
            + [pl.BlockSpec(memory_space=pl.ANY)] * len(pieces),
            out_specs=pl.BlockSpec((1, classes, rows), lambda y, _: (y, 0, 0)),
            scratch_shapes=[
                pltpu.VMEM((TILES, classes, rows), BF),
                pltpu.SemaphoreType.DMA((len(pieces),)),
            ],
        ),
        out_shape=jax.ShapeDtypeStruct(prior.shape, BF),
        compiler_params=pltpu.CompilerParams(vmem_limit_bytes=24 << 20),
        cost_estimate=pl.CostEstimate(
            flops=2 * ny * rows * NT * TILE * classes * 4,
            bytes_accessed=weights.size * 2 + 4 * prior.size * 2,
            transcendentals=0,
        ),
    )(index, weights, prior, *pieces)


def around_x(mine):
    forward = [(i, (i + 1) % NX) for i in range(NX)]
    backward = [(i, (i - 1) % NX) for i in range(NX)]
    before = lax.ppermute(mine, "x", forward)
    after = lax.ppermute(mine, "x", backward)
    half = NY // 2
    oppa = lax.ppermute(before[:half], "x", forward)
    oppb = lax.ppermute(after[half:], "x", backward)
    return mine, after, oppa, oppb, before


def on_device(features, class_bias, logits, tile_lists, valid_counts):
    width = features.shape[1]
    rows, classes = logits.shape
    z, core, x = lax.axis_index("z"), lax.axis_index("c"), lax.axis_index("x")

    owners = tile_lists.reshape(PER)
    order = jnp.arange(PER, dtype=jnp.int32)
    same = (owners[:, None] == owners[None, :]) & (order[None, :] < order[:, None])
    position = owners * 2 + jnp.sum(same.astype(jnp.int32), axis=1)
    hits = position.reshape(NBLK, NT)[:, :, None] == jnp.arange(SLOTS, dtype=jnp.int32)
    hits = hits.astype(BF)

    row = core * ROWS_C + z * SUB
    mine = lax.dynamic_slice_in_dim(features.reshape(NBLK, QB, width), row, SUB, axis=1)
    outgoing = jnp.einsum(
        "bs,bf->sf",
        hits.sum(axis=1),
        mine.reshape(NBLK, SUB * width),
        preferred_element_type=F32,
    ).astype(BF)
    arrived = lax.all_to_all(
        outgoing.reshape(TILES, 2 * SUB, width), ("x", "y"), 0, 0, tiled=True
    )

    adjusted = logits.astype(F32) + class_bias[None, :]
    part = jnp.sum(jnp.exp(adjusted), axis=1)
    parts = lax.all_to_all(
        jnp.broadcast_to(part, (NZ * NC, rows)), ("z", "c"), 0, 0, tiled=True
    )
    totals = jnp.sum(parts, axis=0)
    prior = (jnp.exp(adjusted) / totals[:, None]).astype(BF)
    prior = prior.T.reshape(NY, classes // NY, rows)
    prior = lax.all_to_all(prior, "y", 0, 0, tiled=True)

    memory = unitnorm_rows(features)
    queries = unitnorm_rows(arrived.reshape(SLOTS * SUB, width))
    scores = lax.dot_general(
        queries, memory, (((1,), (1,)), ((), ())), preferred_element_type=F32
    ) / SOFTMAX_TEMPER
    columns = jnp.arange(TILE, dtype=jnp.int32)
    scored = jnp.where(columns < valid_counts[0], jnp.exp(scores), 0.0).astype(BF)
    back = lax.all_to_all(
        scored.reshape(TILES, 2 * SUB, TILE), ("x", "y"), 0, 0, tiled=True
    ).reshape(SLOTS, SUB * TILE)
    chosen = jnp.einsum("bks,sf->bkf", hits, back, preferred_element_type=F32)
    chosen = chosen.reshape(NBLK, NT, SUB, TILE)
    denominator = jnp.sum(chosen, axis=(1, 3), keepdims=True)
    scaled = (ALPHA * chosen / denominator).astype(BF)
    scaled = scaled.transpose(0, 2, 1, 3).reshape(NBLK, SUB, NT * TILE)

    over_z = lax.all_to_all(
        jnp.broadcast_to(scaled, (NZ,) + scaled.shape), "z", 0, 0, tiled=True
    )
    over_z = over_z.transpose(1, 0, 2, 3).reshape(NBLK * ROWS_C, NT * TILE)
    names = jnp.zeros((16, NT * TILE), BF).at[0, :PER].set(owners.astype(BF))
    piece = jnp.concatenate([over_z, names], axis=0)
    weights = lax.all_gather(piece, ("y", "c"), axis=0, tiled=False)

    named = weights[::NC, NBLK * ROWS_C, :PER].astype(jnp.int32)
    index = ((named // NY - x) % NX) * NY + named % NY
    index = index.reshape(NY * PER)

    labels = sweep(index, weights, prior, around_x(prior))
    spread = sweep(index, weights, prior, around_x(labels))
    spread = lax.all_to_all(spread, "y", 0, 0, tiled=True)
    return jnp.log(spread.reshape(classes, rows).T.astype(F32))


def solution(mesh):
    split = Mesh(mesh.devices.reshape(NX, NY, NZ, NC), ("x", "y", "z", "c"))
    dp, tensor = ("x", "y"), ("z", "c")
    in_specs = (P(dp, None), P(tensor), P(dp, tensor), P(dp, None), P(dp))
    return jax.shard_map(
        on_device, mesh=split, in_specs=in_specs, out_specs=P(dp, tensor), check_vma=False
    )
```

```python
import math

import jax
import jax.numpy as jnp
from jax import lax
from jax.experimental import pallas as pl
from jax.experimental.pallas import tpu as pltpu
from jax.sharding import Mesh
from jax.sharding import PartitionSpec as P

ALPHA = 0.75
SOFTMAX_TEMPER = 0.05
EPSILON = 1e-06

NX, NY, NZ, NC = 4, 8, 8, 2
TILES = NX * NY
TILE = 512
QB = 32
NBLK = 16
NT = 2
PER = NBLK * NT
SLOTS = TILES * 2
SUB = 2
ROWS_C = QB // NC
BF = jnp.bfloat16
F32 = jnp.float32


def unitnorm_rows(features):
    wide = features.astype(F32)
    scale = lax.rsqrt(jnp.mean(wide * wide, axis=-1, keepdims=True) + EPSILON)
    return (wide * scale / math.sqrt(wide.shape[-1])).astype(BF)


def sweep_kernel(index_ref, me_ref, w_ref, prior_ref, own, after, oppa, oppb, before, out_ref, held, sems):
    y = pl.program_id(0)

    @pl.when(y == 0)
    def _():
        half = NY // 2
        places = (
            (own, 0, NY),
            (after, NY, NY),
            (oppa, 2 * NY, half),
            (oppb, 2 * NY + half, half),
            (before, 3 * NY, NY),
        )
        copies = [
            pltpu.make_async_copy(src, held.at[pl.ds(at, n)], sems.at[i])
            for i, (src, at, n) in enumerate(places)
        ]
        for copy in copies:
            copy.start()
        for copy in copies:
            copy.wait()

    classes = out_ref.shape[1]
    lanes = lax.broadcasted_iota(jnp.int32, (classes, 128), 1) // QB
    for group in range(NBLK // 4):
        total = None
        for k in range(NT):
            weights = jnp.concatenate(
                [
                    w_ref[c, pl.ds((4 * group + b) * ROWS_C, ROWS_C), pl.ds(k * TILE, TILE)]
                    for b in range(4)
                    for c in range(NC)
                ],
                axis=0,
            )
            labels = jnp.concatenate(
                [held[index_ref[y * PER + (4 * group + b) * NT + k]] for b in range(4)], axis=0
            )
            sums = lax.dot_general(
                labels, weights, (((1,), (1,)), ((), ())), preferred_element_type=F32
            )
            total = sums if total is None else total + sums
        picked = total[:classes]
        for b in range(1, 4):
            picked = jnp.where(lanes == b, total[b * classes : (b + 1) * classes], picked)
        at = pl.ds(128 * group, 128)
        prior = prior_ref[0, :, at].astype(F32)
        out_ref[0, :, at] = (picked + (1.0 - ALPHA) * prior).astype(BF)


def sweep(index, me, weights, prior, pieces):
    ny, classes, rows = prior.shape
    return pl.pallas_call(
        sweep_kernel,
        grid_spec=pltpu.PrefetchScalarGridSpec(
            num_scalar_prefetch=2,
            grid=(ny,),
            in_specs=[
                pl.BlockSpec((NC,) + weights.shape[1:], lambda y, _, me: (y, 0, 0)),
                pl.BlockSpec((1, classes, rows), lambda y, _, me: ((me[0] - y + NY) % NY, 0, 0)),
            ]
            + [pl.BlockSpec(memory_space=pl.ANY)] * len(pieces),
            out_specs=pl.BlockSpec((1, classes, rows), lambda y, _, me: (y, 0, 0)),
            scratch_shapes=[
                pltpu.VMEM((TILES, classes, rows), BF),
                pltpu.SemaphoreType.DMA((len(pieces),)),
            ],
        ),
        out_shape=jax.ShapeDtypeStruct(prior.shape, BF),
        compiler_params=pltpu.CompilerParams(vmem_limit_bytes=24 << 20),
        cost_estimate=pl.CostEstimate(
            flops=2 * ny * rows * NT * TILE * classes * 4,
            bytes_accessed=weights.size * 2 + 4 * prior.size * 2,
            transcendentals=0,
        ),
    )(index, me, weights, prior, *pieces)


def around_x(mine):
    forward = [(i, (i + 1) % NX) for i in range(NX)]
    backward = [(i, (i - 1) % NX) for i in range(NX)]
    before = lax.ppermute(mine, "x", forward)
    after = lax.ppermute(mine, "x", backward)
    half = NY // 2
    oppa = lax.ppermute(before[:half], "x", forward)
    oppb = lax.ppermute(after[half:], "x", backward)
    return mine, after, oppa, oppb, before


def over_y(pieces):
    y = lax.axis_index("y")
    turned = lax.dynamic_slice_in_dim(jnp.concatenate([pieces, pieces]), y, NY, axis=0)
    got = [turned[0]]
    for d in range(1, NY):
        got.append(lax.ppermute(turned[d], "y", [(i, (i + d) % NY) for i in range(NY)]))
    return jnp.stack(got)


def turned_totals(totals):
    x, y = lax.axis_index("x"), lax.axis_index("y")
    grid = totals.reshape(NX, NY, -1)
    grid = lax.dynamic_slice_in_dim(jnp.concatenate([grid, grid], axis=0), x, NX, axis=0)
    grid = jnp.flip(grid, axis=1)
    return lax.dynamic_slice_in_dim(
        jnp.concatenate([grid, grid], axis=1), NY - 1 - y, NY, axis=1
    )


def on_device(features, class_bias, logits, tile_lists, valid_counts):
    width = features.shape[1]
    rows, classes = logits.shape
    x, y = lax.axis_index("x"), lax.axis_index("y")
    z, core = lax.axis_index("z"), lax.axis_index("c")

    owners = tile_lists.reshape(PER)
    order = jnp.arange(PER, dtype=jnp.int32)
    same = (owners[:, None] == owners[None, :]) & (order[None, :] < order[:, None])
    position = owners * 2 + jnp.sum(same.astype(jnp.int32), axis=1)
    hits = position.reshape(NBLK, NT)[:, :, None] == jnp.arange(SLOTS, dtype=jnp.int32)
    hits = hits.astype(BF)

    row = core * ROWS_C + z * SUB
    mine = lax.dynamic_slice_in_dim(features.reshape(NBLK, QB, width), row, SUB, axis=1)
    outgoing = jnp.einsum(
        "bs,bf->sf",
        hits.sum(axis=1),
        mine.reshape(NBLK, SUB * width),
        preferred_element_type=F32,
    ).astype(BF)
    outgoing, raw = lax.optimization_barrier((outgoing, logits))
    arrived = lax.all_to_all(
        outgoing.reshape(TILES, 2 * SUB, width), ("x", "y"), 0, 0, tiled=True
    )

    raw = over_y(raw.T.reshape(NY, classes // NY, rows))

    memory = unitnorm_rows(features)
    queries = unitnorm_rows(arrived.reshape(SLOTS * SUB, width))
    scores = lax.dot_general(
        queries, memory, (((1,), (1,)), ((), ())), preferred_element_type=F32
    ) / SOFTMAX_TEMPER
    columns = jnp.arange(TILE, dtype=jnp.int32)
    scored = jnp.where(columns < valid_counts[0], jnp.exp(scores), 0.0).astype(BF)
    scored, raw = lax.optimization_barrier((scored, raw))
    raw = around_x(raw)
    back = lax.all_to_all(
        scored.reshape(TILES, 2 * SUB, TILE), ("x", "y"), 0, 0, tiled=True
    ).reshape(SLOTS, SUB * TILE)
    chosen = jnp.einsum("bks,sf->bkf", hits, back, preferred_element_type=F32)
    chosen = chosen.reshape(NBLK, NT, SUB, TILE)
    denominator = jnp.sum(chosen, axis=(1, 3), keepdims=True)
    scaled = (ALPHA * chosen / denominator).astype(BF)
    scaled = scaled.transpose(0, 2, 1, 3).reshape(NBLK, SUB, NT * TILE)

    over_z = lax.all_to_all(
        jnp.broadcast_to(scaled, (NZ,) + scaled.shape), "z", 0, 0, tiled=True
    )
    over_z, after, before = lax.optimization_barrier((over_z, raw[1], raw[4]))
    raw = raw[0], after, raw[2], raw[3], before
    over_z = over_z.transpose(1, 0, 2, 3).reshape(NBLK * ROWS_C, NT * TILE)
    names = jnp.zeros((16, NT * TILE), BF).at[0, :PER].set(owners.astype(BF))
    piece = jnp.concatenate([over_z, names], axis=0)
    weights = lax.all_gather(piece, ("y", "c"), axis=0, tiled=False)

    adjusted = logits.astype(F32) + class_bias[None, :]
    part = jnp.sum(jnp.exp(adjusted), axis=1)
    part, _ = lax.optimization_barrier((part, piece))
    parts = lax.all_to_all(
        jnp.broadcast_to(part, (NZ * NC, rows)), ("z", "c"), 0, 0, tiled=True
    )
    totals = jnp.sum(parts, axis=0)
    totals = lax.all_to_all(
        jnp.broadcast_to(totals, (TILES, rows)), ("x", "y"), 0, 0, tiled=True
    )
    totals = turned_totals(totals)

    bias = lax.dynamic_slice_in_dim(class_bias.reshape(NY, classes // NY), y, 1, axis=0)
    bias = bias.reshape(1, classes // NY, 1)
    half = NY // 2
    sums = totals[0], totals[1], totals[2, :half], totals[2, half:], totals[3]
    priors = tuple(
        (jnp.exp(r.astype(F32) + bias) / t[:, None, :]).astype(BF) for r, t in zip(raw, sums)
    )

    named = weights[::NC, NBLK * ROWS_C, :PER].astype(jnp.int32).reshape(NY * PER)
    at_x, at_y = (named // NY - x) % NX * NY, named % NY
    me = y.reshape(1)

    labels = sweep(at_x + (y - at_y) % NY, me, weights, priors[0], priors)
    spread = sweep(at_x + at_y, me, weights, priors[0], around_x(labels))
    spread = lax.all_to_all(spread, "y", 0, 0, tiled=True)
    return jnp.log(spread.reshape(classes, rows).T.astype(F32))


def solution(mesh):
    split = Mesh(mesh.devices.reshape(NX, NY, NZ, NC), ("x", "y", "z", "c"))
    dp, tensor = ("x", "y"), ("z", "c")
    in_specs = (P(dp, None), P(tensor), P(dp, tensor), P(dp, None), P(dp))
    return jax.shard_map(
        on_device, mesh=split, in_specs=in_specs, out_specs=P(dp, tensor), check_vma=False
    )
```

```python
import functools
import math

import jax
import jax.numpy as jnp
from jax import lax
from jax.experimental import pallas as pl
from jax.experimental.pallas import tpu as pltpu
from jax.sharding import Mesh
from jax.sharding import PartitionSpec as P

ALPHA = 0.75
SOFTMAX_TEMPER = 0.05
EPSILON = 1e-06

NX, NY, NZ, NC = 4, 8, 8, 2
TILES = NX * NY
TILE = 512
QB = 32
NBLK = 16
NT = 2
PER = NBLK * NT
SLOTS = TILES * 2
SUB = 2
PARTS = 2
BF = jnp.bfloat16
F32 = jnp.float32


def unitnorm_rows(features):
    wide = features.astype(F32)
    scale = lax.rsqrt(jnp.mean(wide * wide, axis=-1, keepdims=True) + EPSILON)
    return (wide * scale / math.sqrt(wide.shape[-1])).astype(BF)


def sweep_kernel(first, counts, index_ref, *refs):
    n_weights, n_labels = counts
    w_refs, prior_ref, refs = refs[:n_weights], refs[n_weights], refs[n_weights + 1 :]
    labels_refs, (out_ref, held, sems) = refs[: 5 * n_labels], refs[5 * n_labels :]
    y = pl.program_id(0)

    @pl.when(y == 0)
    def _():
        half, lanes = NY // 2, TILE // n_labels
        at = (0, NY, 2 * NY, 2 * NY + half, 3 * NY)
        copies = []
        for i, src in enumerate(labels_refs):
            part, piece = divmod(i, 5)
            dst = held.at[
                pl.ds(at[piece], src.shape[0]), :, pl.ds(part * lanes, lanes)
            ]
            copies.append(pltpu.make_async_copy(src, dst, sems.at[i]))
        for copy in copies:
            copy.start()
        for copy in copies:
            copy.wait()

    classes = out_ref.shape[1]
    lanes = lax.broadcasted_iota(jnp.int32, (classes, 128), 1) // QB
    per_part = w_refs[0].shape[1] * NC // QB
    for group in range(n_weights * per_part // 4):
        part, local = divmod(group * 4, per_part)
        total = None
        for k in range(NT):
            weights = block_rows(w_refs[part], local, per_part, k)
            labels = jnp.concatenate(
                [held[index_ref[y * PER + (first + 4 * group + b) * NT + k]] for b in range(4)],
                axis=0,
            )
            sums = lax.dot_general(
                labels, weights, (((1,), (1,)), ((), ())), preferred_element_type=F32
            )
            total = sums if total is None else total + sums
        picked = total[:classes]
        for b in range(1, 4):
            picked = jnp.where(lanes == b, total[b * classes : (b + 1) * classes], picked)
        at = pl.ds(128 * group, 128)
        prior = prior_ref[0, :, at].astype(F32)
        out_ref[0, :, at] = (picked + (1.0 - ALPHA) * prior).astype(BF)


def block_rows(w_ref, block, per_part, k):
    each = per_part // NC
    core, at = divmod(block, each)
    columns = pl.ds(k * TILE, TILE)
    if at + 4 <= each:
        return w_ref[core, pl.ds(at * QB, 4 * QB), columns]
    return jnp.concatenate(
        [w_ref[(block + b) // each, pl.ds((block + b) % each * QB, QB), columns] for b in range(4)],
        axis=0,
    )


def sweep(index, weights, first, prior, lane_block, pieces):
    ny, classes, _ = prior.shape
    rows = len(weights) * NC * weights[0].shape[1]
    flat = [piece for part in pieces for piece in part]
    return pl.pallas_call(
        functools.partial(sweep_kernel, first, (len(weights), len(pieces))),
        grid_spec=pltpu.PrefetchScalarGridSpec(
            num_scalar_prefetch=1,
            grid=(ny,),
            in_specs=[
                pl.BlockSpec((NC,) + w.shape[1:], lambda y, _: (y, 0, 0)) for w in weights
            ]
            + [pl.BlockSpec((1, classes, rows), lambda y, _: (y, 0, lane_block))]
            + [pl.BlockSpec(memory_space=pl.ANY)] * len(flat),
            out_specs=pl.BlockSpec((1, classes, rows), lambda y, _: (y, 0, 0)),
            scratch_shapes=[
                pltpu.VMEM((TILES, classes, TILE), BF),
                pltpu.SemaphoreType.DMA((len(flat),)),
            ],
        ),
        out_shape=jax.ShapeDtypeStruct((ny, classes, rows), BF),
        compiler_params=pltpu.CompilerParams(vmem_limit_bytes=40 << 20),
        cost_estimate=pl.CostEstimate(
            flops=2 * ny * rows * NT * TILE * classes * 4,
            bytes_accessed=sum(w.size for w in weights) * 2 + 4 * prior.size * 2,
            transcendentals=0,
        ),
    )(index, *weights, prior, *flat)


def around_x(mine):
    forward = [(i, (i + 1) % NX) for i in range(NX)]
    backward = [(i, (i - 1) % NX) for i in range(NX)]
    before = lax.ppermute(mine, "x", forward)
    after = lax.ppermute(mine, "x", backward)
    half = NY // 2
    oppa = lax.ppermute(before[:half], "x", forward)
    oppb = lax.ppermute(after[half:], "x", backward)
    return mine, after, oppa, oppb, before


def on_device(features, class_bias, logits, tile_lists, valid_counts):
    width = features.shape[1]
    rows, classes = logits.shape
    z, core, x = lax.axis_index("z"), lax.axis_index("c"), lax.axis_index("x")

    owners = tile_lists.reshape(PER)
    order = jnp.arange(PER, dtype=jnp.int32)
    same = (owners[:, None] == owners[None, :]) & (order[None, :] < order[:, None])
    position = owners * 2 + jnp.sum(same.astype(jnp.int32), axis=1)
    hits = position.reshape(NBLK, NT)[:, :, None] == jnp.arange(SLOTS, dtype=jnp.int32)
    hits = hits.astype(BF)

    row = (z * NC + core) * SUB
    mine = lax.dynamic_slice_in_dim(features.reshape(NBLK, QB, width), row, SUB, axis=1)
    outgoing = jnp.einsum(
        "bs,bf->sf",
        hits.sum(axis=1),
        mine.reshape(NBLK, SUB * width),
        preferred_element_type=F32,
    ).astype(BF)
    arrived = lax.all_to_all(
        outgoing.reshape(TILES, 2 * SUB, width), ("x", "y"), 0, 0, tiled=True
    )

    adjusted = logits.astype(F32) + class_bias[None, :]
    part = jnp.sum(jnp.exp(adjusted), axis=1)
    parts = lax.all_to_all(
        jnp.broadcast_to(part, (NZ * NC, rows)), ("z", "c"), 0, 0, tiled=True
    )
    totals = jnp.sum(parts, axis=0)
    prior = (jnp.exp(adjusted) / totals[:, None]).astype(BF)
    prior = prior.T.reshape(NY, classes // NY, rows)
    prior = lax.all_to_all(prior, "y", 0, 0, tiled=True)
    lists = lax.all_to_all(
        jnp.broadcast_to(owners, (NY, PER)), "y", 0, 0, tiled=True
    )

    memory = unitnorm_rows(features)
    queries = unitnorm_rows(arrived.reshape(SLOTS * SUB, width))
    scores = lax.dot_general(
        queries, memory, (((1,), (1,)), ((), ())), preferred_element_type=F32
    ) / SOFTMAX_TEMPER
    columns = jnp.arange(TILE, dtype=jnp.int32)
    scored = jnp.where(columns < valid_counts[0], jnp.exp(scores), 0.0).astype(BF)
    back = lax.all_to_all(
        scored.reshape(TILES, 2 * SUB, TILE), ("x", "y"), 0, 0, tiled=True
    ).reshape(SLOTS, SUB * TILE)
    chosen = jnp.einsum("bks,sf->bkf", hits, back, preferred_element_type=F32)
    chosen = chosen.reshape(NBLK, NT, SUB, TILE)
    denominator = jnp.sum(chosen, axis=(1, 3), keepdims=True)
    scaled = (ALPHA * chosen / denominator).astype(BF)
    scaled = scaled.transpose(0, 2, 1, 3).reshape(NBLK, SUB, NT * TILE)

    own = lax.all_gather(scaled, ("z", "c"), axis=0, tiled=False)
    own, prior = lax.optimization_barrier((own, prior))
    count = NBLK // PARTS // NC
    gathered = []
    for part in range(PARTS):
        piece = lax.dynamic_slice_in_dim(own, (part * NC + core) * count, count, axis=1)
        piece = piece.transpose(1, 0, 2, 3).reshape(count * QB, NT * TILE)
        gathered.append(lax.all_gather(piece, ("y", "c"), axis=0, tiled=False))

    named = lists.reshape(NY * PER)
    index = (named // NY - x) % NX * NY + named % NY

    priors = around_x(prior)
    each = [
        sweep(index, [w], part * NBLK // PARTS, prior, part, [priors])
        for part, w in enumerate(gathered)
    ]
    spread = sweep(index, gathered, 0, prior, 0, [around_x(labels) for labels in each])
    spread = lax.all_to_all(spread, "y", 0, 0, tiled=True)
    return jnp.log(spread.reshape(classes, rows).T.astype(F32))


def solution(mesh):
    split = Mesh(mesh.devices.reshape(NX, NY, NZ, NC), ("x", "y", "z", "c"))
    dp, tensor = ("x", "y"), ("z", "c")
    in_specs = (P(dp, None), P(tensor), P(dp, tensor), P(dp, None), P(dp))
    return jax.shard_map(
        on_device, mesh=split, in_specs=in_specs, out_specs=P(dp, tensor), check_vma=False
    )
```

```python
import functools
import math

import jax
import jax.numpy as jnp
from jax import lax
from jax.experimental import pallas as pl
from jax.experimental.pallas import tpu as pltpu
from jax.sharding import Mesh
from jax.sharding import PartitionSpec as P

ALPHA = 0.75
SOFTMAX_TEMPER = 0.05
EPSILON = 1e-06

NX, NY, NZ, NC = 4, 8, 8, 2
TILES = NX * NY
TILE = 512
QB = 32
NBLK = 16
NT = 2
PER = NBLK * NT
SLOTS = TILES * 2
SUB = 2
BF = jnp.bfloat16
F32 = jnp.float32


def unitnorm_rows(features):
    wide = features.astype(F32)
    scale = lax.rsqrt(jnp.mean(wide * wide, axis=-1, keepdims=True) + EPSILON)
    return (wide * scale / math.sqrt(wide.shape[-1])).astype(BF)


def sweep_kernel(first, counts, index_ref, *refs):
    n_weights, n_labels = counts
    w_refs, prior_ref, refs = refs[:n_weights], refs[n_weights], refs[n_weights + 1 :]
    labels_refs, (out_ref, held, sems) = refs[: 5 * n_labels], refs[5 * n_labels :]
    y = pl.program_id(0)

    @pl.when(y == 0)
    def _():
        half, lanes = NY // 2, TILE // n_labels
        at = (0, NY, 2 * NY, 2 * NY + half, 3 * NY)
        copies = []
        for i, src in enumerate(labels_refs):
            part, piece = divmod(i, 5)
            dst = held.at[
                pl.ds(at[piece], src.shape[0]), :, pl.ds(part * lanes, lanes)
            ]
            copies.append(pltpu.make_async_copy(src, dst, sems.at[i]))
        for copy in copies:
            copy.start()
        for copy in copies:
            copy.wait()

    classes = out_ref.shape[1]
    lanes = lax.broadcasted_iota(jnp.int32, (classes, 128), 1) // QB
    per_part = w_refs[0].shape[1] * NC // QB
    for group in range(n_weights * per_part // 4):
        part, local = divmod(group * 4, per_part)
        total = None
        for k in range(NT):
            weights = block_rows(w_refs[part], local, per_part, k)
            labels = jnp.concatenate(
                [held[index_ref[y * PER + (first + 4 * group + b) * NT + k]] for b in range(4)],
                axis=0,
            )
            sums = lax.dot_general(
                labels, weights, (((1,), (1,)), ((), ())), preferred_element_type=F32
            )
            total = sums if total is None else total + sums
        picked = total[:classes]
        for b in range(1, 4):
            picked = jnp.where(lanes == b, total[b * classes : (b + 1) * classes], picked)
        at = pl.ds(128 * group, 128)
        prior = prior_ref[0, :, at].astype(F32)
        out_ref[0, :, at] = (picked + (1.0 - ALPHA) * prior).astype(BF)


def block_rows(w_ref, block, per_part, k):
    each = per_part // NC
    core, at = divmod(block, each)
    columns = pl.ds(k * TILE, TILE)
    if at + 4 <= each:
        return w_ref[core, pl.ds(at * QB, 4 * QB), columns]
    return jnp.concatenate(
        [w_ref[(block + b) // each, pl.ds((block + b) % each * QB, QB), columns] for b in range(4)],
        axis=0,
    )


def sweep(index, weights, first, prior, lane_block, pieces):
    ny, classes, _ = prior.shape
    rows = len(weights) * NC * weights[0].shape[1]
    flat = [piece for part in pieces for piece in part]
    return pl.pallas_call(
        functools.partial(sweep_kernel, first, (len(weights), len(pieces))),
        grid_spec=pltpu.PrefetchScalarGridSpec(
            num_scalar_prefetch=1,
            grid=(ny,),
            in_specs=[
                pl.BlockSpec((NC,) + w.shape[1:], lambda y, _: (y, 0, 0)) for w in weights
            ]
            + [pl.BlockSpec((1, classes, rows), lambda y, _: (y, 0, lane_block))]
            + [pl.BlockSpec(memory_space=pl.ANY)] * len(flat),
            out_specs=pl.BlockSpec((1, classes, rows), lambda y, _: (y, 0, 0)),
            scratch_shapes=[
                pltpu.VMEM((TILES, classes, TILE), BF),
                pltpu.SemaphoreType.DMA((len(flat),)),
            ],
        ),
        out_shape=jax.ShapeDtypeStruct((ny, classes, rows), BF),
        compiler_params=pltpu.CompilerParams(vmem_limit_bytes=48 << 20),
        cost_estimate=pl.CostEstimate(
            flops=2 * ny * rows * NT * TILE * classes * 4,
            bytes_accessed=sum(w.size for w in weights) * 2 + 4 * prior.size * 2,
            transcendentals=0,
        ),
    )(index, *weights, prior, *flat)


def around_x(mine):
    forward = [(i, (i + 1) % NX) for i in range(NX)]
    backward = [(i, (i - 1) % NX) for i in range(NX)]
    before = lax.ppermute(mine, "x", forward)
    after = lax.ppermute(mine, "x", backward)
    half = NY // 2
    oppa = lax.ppermute(before[:half], "x", forward)
    oppb = lax.ppermute(after[half:], "x", backward)
    return mine, after, oppa, oppb, before


def split_terms(value):
    terms = []
    for scale in (0.99, 1.0, 1.0):
        term = (value * scale).astype(BF)
        value = value - term.astype(F32)
        terms.append(term)
    return terms


def on_device(features, class_bias, logits, tile_lists, valid_counts):
    width = features.shape[1]
    rows, classes = logits.shape
    x, y = lax.axis_index("x"), lax.axis_index("y")
    z, core = lax.axis_index("z"), lax.axis_index("c")

    owners = tile_lists.reshape(PER)
    order = jnp.arange(PER, dtype=jnp.int32)
    same = (owners[:, None] == owners[None, :]) & (order[None, :] < order[:, None])
    position = owners * 2 + jnp.sum(same.astype(jnp.int32), axis=1)
    hits = position.reshape(NBLK, NT)[:, :, None] == jnp.arange(SLOTS, dtype=jnp.int32)
    hits = hits.astype(BF)

    row = (z * NC + core) * SUB
    mine = lax.dynamic_slice_in_dim(features.reshape(NBLK, QB, width), row, SUB, axis=1)
    outgoing = jnp.einsum(
        "bs,bf->sf",
        hits.sum(axis=1),
        mine.reshape(NBLK, SUB * width),
        preferred_element_type=F32,
    ).astype(BF)
    arrived = lax.all_to_all(
        outgoing.reshape(TILES, 2 * SUB, width), ("x", "y"), 0, 0, tiled=True
    )

    memory = unitnorm_rows(features)
    queries = unitnorm_rows(arrived.reshape(SLOTS * SUB, width))
    scores = lax.dot_general(
        queries, memory, (((1,), (1,)), ((), ())), preferred_element_type=F32
    ) / SOFTMAX_TEMPER
    columns = jnp.arange(TILE, dtype=jnp.int32)
    scored = jnp.where(columns < valid_counts[0], jnp.exp(scores), 0.0).astype(BF)
    back = lax.all_to_all(
        scored.reshape(TILES, 2 * SUB, TILE), ("x", "y"), 0, 0, tiled=True
    ).reshape(SLOTS, SUB * TILE)
    chosen = jnp.einsum("bks,sf->bkf", hits, back, preferred_element_type=F32)
    chosen = chosen.reshape(NBLK, NT, SUB, TILE)
    denominator = jnp.sum(chosen, axis=(1, 3), keepdims=True)
    scaled = (ALPHA * chosen / denominator).astype(BF)
    scaled = scaled.transpose(0, 2, 1, 3).reshape(NBLK, SUB, NT * TILE)

    part = jnp.sum(jnp.exp(logits.astype(F32) + class_bias[None, :]), axis=1)
    high, middle, low = split_terms(part)
    terms = jnp.concatenate([high, middle, low, jnp.zeros_like(low)])
    piece = jnp.concatenate([scaled, terms.reshape(1, SUB, NT * TILE)])
    own = lax.all_gather(piece, ("z", "c"), axis=0, tiled=False)

    raw, _ = lax.optimization_barrier((logits, piece))
    raw = raw.T.reshape(NY, classes // NY, rows)
    raw = lax.all_to_all(raw, "y", 0, 0, tiled=True)
    own, _ = lax.optimization_barrier((own, raw))
    raw = around_x(raw)

    half = NBLK // NC
    piece = lax.dynamic_slice_in_dim(own, core * half, half, axis=1)
    piece = piece.transpose(1, 0, 2, 3).reshape(half * QB, NT * TILE)
    weights = lax.all_gather(piece, ("y", "c"), axis=0, tiled=False)

    terms = jnp.sum(own[:, NBLK].astype(F32), axis=0).reshape(4, rows)
    totals = terms[0] + terms[1] + terms[2]
    known = jnp.concatenate([totals, owners.astype(F32), jnp.zeros((128 - PER,), F32)])
    known = lax.all_to_all(
        jnp.broadcast_to(known, (TILES,) + known.shape), ("x", "y"), 0, 0, tiled=True
    )
    known = known.reshape(NX, NY, -1)
    known = lax.dynamic_slice_in_dim(jnp.concatenate([known, known]), x, NX, axis=0)
    totals = known[:, :, :rows]

    bias = lax.dynamic_slice_in_dim(class_bias.reshape(NY, classes // NY), y, 1, axis=0)
    bias = bias.reshape(1, classes // NY, 1)
    half = NY // 2
    sums = totals[0], totals[1], totals[2, :half], totals[2, half:], totals[3]
    priors = tuple(
        (jnp.exp(r.astype(F32) + bias) / t[:, None, :]).astype(BF) for r, t in zip(raw, sums)
    )

    named = known[0, :, rows : rows + PER].astype(jnp.int32).reshape(NY * PER)
    index = (named // NY - x) % NX * NY + named % NY

    labels = sweep(index, [weights], 0, priors[0], 0, [priors])
    spread = sweep(index, [weights], 0, priors[0], 0, [around_x(labels)])
    spread = lax.all_to_all(spread, "y", 0, 0, tiled=True)
    return jnp.log(spread.reshape(classes, rows).T.astype(F32))


def solution(mesh):
    split = Mesh(mesh.devices.reshape(NX, NY, NZ, NC), ("x", "y", "z", "c"))
    dp, tensor = ("x", "y"), ("z", "c")
    in_specs = (P(dp, None), P(tensor), P(dp, tensor), P(dp, None), P(dp))
    return jax.shard_map(
        on_device, mesh=split, in_specs=in_specs, out_specs=P(dp, tensor), check_vma=False
    )
```

```python
import math

import jax
import jax.numpy as jnp
from jax import lax
from jax.experimental import pallas as pl
from jax.experimental.pallas import tpu as pltpu
from jax.sharding import Mesh
from jax.sharding import PartitionSpec as P

ALPHA = 0.75
SOFTMAX_TEMPER = 0.05
EPSILON = 1e-06

NX, NY, NZ, NC = 4, 8, 8, 2
TILES = NX * NY
TILE = 512
QB = 32
NBLK = 16
NT = 2
PER = NBLK * NT
SLOTS = TILES * 2
SUB = 2
ROWS_C = QB // NC
BF = jnp.bfloat16
F32 = jnp.float32


def unitnorm_rows(features):
    wide = features.astype(F32)
    scale = lax.rsqrt(jnp.mean(wide * wide, axis=-1, keepdims=True) + EPSILON)
    return (wide * scale / math.sqrt(wide.shape[-1])).astype(BF)


def sweep_kernel(index_ref, mine_ref, other_ref, prior_ref, own, after, oppa, oppb, before, out_ref, held, sems):
    y = pl.program_id(0)

    @pl.when(y == 0)
    def _():
        half = NY // 2
        places = (
            (own, 0, NY),
            (after, NY, NY),
            (oppa, 2 * NY, half),
            (oppb, 2 * NY + half, half),
            (before, 3 * NY, NY),
        )
        copies = [
            pltpu.make_async_copy(src, held.at[pl.ds(at, n)], sems.at[i])
            for i, (src, at, n) in enumerate(places)
        ]
        for copy in copies:
            copy.start()
        for copy in copies:
            copy.wait()

    first_core = index_ref[NY * PER] == 0
    classes = out_ref.shape[1]
    lanes = lax.broadcasted_iota(jnp.int32, (classes, 128), 1) // QB
    for group in range(NBLK // 4):
        total = None
        for k in range(NT):
            rows = []
            for b in range(4):
                at = pl.ds((4 * group + b) * ROWS_C, ROWS_C), pl.ds(k * TILE, TILE)
                mine, other = mine_ref[0, *at], other_ref[0, *at]
                rows.append(jnp.where(first_core, mine, other))
                rows.append(jnp.where(first_core, other, mine))
            weights = jnp.concatenate(rows, axis=0)
            labels = jnp.concatenate(
                [held[index_ref[y * PER + (4 * group + b) * NT + k]] for b in range(4)], axis=0
            )
            sums = lax.dot_general(
                labels, weights, (((1,), (1,)), ((), ())), preferred_element_type=F32
            )
            total = sums if total is None else total + sums
        picked = total[:classes]
        for b in range(1, 4):
            picked = jnp.where(lanes == b, total[b * classes : (b + 1) * classes], picked)
        at = pl.ds(128 * group, 128)
        prior = prior_ref[0, :, at].astype(F32)
        out_ref[0, :, at] = (picked + (1.0 - ALPHA) * prior).astype(BF)


def sweep(index, mine, other, prior, pieces):
    ny, classes, rows = prior.shape
    by_y = lambda array: pl.BlockSpec((1,) + array.shape[1:], lambda y, _: (y, 0, 0))
    return pl.pallas_call(
        sweep_kernel,
        grid_spec=pltpu.PrefetchScalarGridSpec(
            num_scalar_prefetch=1,
            grid=(ny,),
            in_specs=[by_y(mine), by_y(other), by_y(prior)]
            + [pl.BlockSpec(memory_space=pl.ANY)] * len(pieces),
            out_specs=by_y(prior),
            scratch_shapes=[
                pltpu.VMEM((TILES, classes, rows), BF),
                pltpu.SemaphoreType.DMA((len(pieces),)),
            ],
        ),
        out_shape=jax.ShapeDtypeStruct(prior.shape, BF),
        compiler_params=pltpu.CompilerParams(vmem_limit_bytes=40 << 20),
        cost_estimate=pl.CostEstimate(
            flops=2 * ny * rows * NT * TILE * classes * 4,
            bytes_accessed=2 * mine.size * 2 + 4 * prior.size * 2,
            transcendentals=0,
        ),
    )(index, mine, other, prior, *pieces)


def around_x(mine):
    forward = [(i, (i + 1) % NX) for i in range(NX)]
    backward = [(i, (i - 1) % NX) for i in range(NX)]
    before = lax.ppermute(mine, "x", forward)
    after = lax.ppermute(mine, "x", backward)
    half = NY // 2
    oppa = lax.ppermute(before[:half], "x", forward)
    oppb = lax.ppermute(after[half:], "x", backward)
    return mine, after, oppa, oppb, before


def split_terms(value):
    terms = []
    for scale in (0.99, 1.0, 1.0):
        term = (value * scale).astype(BF)
        value = value - term.astype(F32)
        terms.append(term)
    return terms


def on_device(features, class_bias, logits, tile_lists, valid_counts):
    width = features.shape[1]
    rows, classes = logits.shape
    x, y = lax.axis_index("x"), lax.axis_index("y")
    z, core = lax.axis_index("z"), lax.axis_index("c")

    raw = logits.T.reshape(NY, classes // NY, rows)
    raw = lax.all_gather(raw, "y", axis=0, tiled=False)

    owners = tile_lists.reshape(PER)
    order = jnp.arange(PER, dtype=jnp.int32)
    same = (owners[:, None] == owners[None, :]) & (order[None, :] < order[:, None])
    position = owners * 2 + jnp.sum(same.astype(jnp.int32), axis=1)
    hits = position.reshape(NBLK, NT)[:, :, None] == jnp.arange(SLOTS, dtype=jnp.int32)
    hits = hits.astype(BF)

    row = core * ROWS_C + z * SUB
    mine = lax.dynamic_slice_in_dim(features.reshape(NBLK, QB, width), row, SUB, axis=1)
    outgoing = jnp.einsum(
        "bs,bf->sf",
        hits.sum(axis=1),
        mine.reshape(NBLK, SUB * width),
        preferred_element_type=F32,
    ).astype(BF)
    arrived = lax.all_to_all(
        outgoing.reshape(TILES, 2 * SUB, width), ("x", "y"), 0, 0, tiled=True
    )

    memory = unitnorm_rows(features)
    queries = unitnorm_rows(arrived.reshape(SLOTS * SUB, width))
    scores = lax.dot_general(
        queries, memory, (((1,), (1,)), ((), ())), preferred_element_type=F32
    ) / SOFTMAX_TEMPER
    columns = jnp.arange(TILE, dtype=jnp.int32)
    scored = jnp.where(columns < valid_counts[0], jnp.exp(scores), 0.0).astype(BF)
    back = lax.all_to_all(
        scored.reshape(TILES, 2 * SUB, TILE), ("x", "y"), 0, 0, tiled=True
    ).reshape(SLOTS, SUB * TILE)
    chosen = jnp.einsum("bks,sf->bkf", hits, back, preferred_element_type=F32)
    chosen = chosen.reshape(NBLK, NT, SUB, TILE)
    denominator = jnp.sum(chosen, axis=(1, 3), keepdims=True)
    scaled = (ALPHA * chosen / denominator).astype(BF)
    scaled = scaled.transpose(0, 2, 1, 3).reshape(NBLK, SUB, NT * TILE)

    part = jnp.sum(jnp.exp(logits.astype(F32) + class_bias[None, :]), axis=1)
    high, middle, low = split_terms(part)
    terms = jnp.concatenate([high, middle, low, jnp.zeros_like(low)])
    piece = jnp.concatenate([scaled, terms.reshape(1, SUB, NT * TILE)])
    over_z = lax.all_to_all(
        jnp.broadcast_to(piece, (NZ,) + piece.shape), "z", 0, 0, tiled=True
    )

    raw, over_z = lax.optimization_barrier((raw, over_z))
    piece = over_z[:, :NBLK].transpose(1, 0, 2, 3).reshape(NBLK * ROWS_C, NT * TILE)
    weights = lax.all_gather(piece, "y", axis=0, tiled=False)

    raw = lax.dynamic_index_in_dim(raw, y, axis=1, keepdims=False)
    raw = around_x(raw)

    terms = jnp.sum(over_z[:, NBLK].astype(F32), axis=0).reshape(4, rows)
    totals = terms[0] + terms[1] + terms[2]
    totals = totals + lax.ppermute(totals, "c", [(0, 1), (1, 0)])
    known = jnp.concatenate([totals, owners.astype(F32), jnp.zeros((128 - PER,), F32)])
    known, _ = lax.optimization_barrier((known, (raw[1], raw[4])))
    known = lax.all_to_all(
        jnp.broadcast_to(known, (TILES,) + known.shape), ("x", "y"), 0, 0, tiled=True
    )
    weights, _ = lax.optimization_barrier((weights, (known, raw)))
    swapped = lax.ppermute(weights, "c", [(0, 1), (1, 0)])
    known = known.reshape(NX, NY, -1)
    known = lax.dynamic_slice_in_dim(jnp.concatenate([known, known]), x, NX, axis=0)
    totals = known[:, :, :rows]

    bias = lax.dynamic_slice_in_dim(class_bias.reshape(NY, classes // NY), y, 1, axis=0)
    bias = bias.reshape(1, classes // NY, 1)
    half = NY // 2
    sums = totals[0], totals[1], totals[2, :half], totals[2, half:], totals[3]
    priors = tuple(
        (jnp.exp(r.astype(F32) + bias) / t[:, None, :]).astype(BF) for r, t in zip(raw, sums)
    )

    named = known[0, :, rows : rows + PER].astype(jnp.int32).reshape(NY * PER)
    index = (named // NY - x) % NX * NY + named % NY
    index = jnp.concatenate([index, core.reshape(1)])

    labels = sweep(index, weights, swapped, priors[0], priors)
    spread = sweep(index, weights, swapped, priors[0], around_x(labels))
    spread = lax.all_to_all(spread, "y", 0, 0, tiled=True)
    return jnp.log(spread.reshape(classes, rows).T.astype(F32))


def solution(mesh):
    split = Mesh(mesh.devices.reshape(NX, NY, NZ, NC), ("x", "y", "z", "c"))
    dp, tensor = ("x", "y"), ("z", "c")
    in_specs = (P(dp, None), P(tensor), P(dp, tensor), P(dp, None), P(dp))
    return jax.shard_map(
        on_device, mesh=split, in_specs=in_specs, out_specs=P(dp, tensor), check_vma=False
    )
```

```python
import math

import jax
import jax.numpy as jnp
from jax import lax
from jax.experimental import pallas as pl
from jax.experimental.pallas import tpu as pltpu
from jax.sharding import Mesh
from jax.sharding import PartitionSpec as P

ALPHA = 0.75
SOFTMAX_TEMPER = 0.05
EPSILON = 1e-06

NX, NY, NZ, NC = 4, 8, 8, 2
TILES = NX * NY
TILE = 512
QB = 32
NBLK = 16
NT = 2
PER = NBLK * NT
SLOTS = TILES * 2
SUB = 2
ROWS_C = QB // NC
BF = jnp.bfloat16
F32 = jnp.float32


def unitnorm_rows(features):
    wide = features.astype(F32)
    scale = lax.rsqrt(jnp.mean(wide * wide, axis=-1, keepdims=True) + EPSILON)
    return (wide * scale / math.sqrt(wide.shape[-1])).astype(BF)


def sweep_kernel(index_ref, w_ref, prior_ref, own, after, oppa, oppb, before, out_ref, held, sems):
    y = pl.program_id(0)

    @pl.when(y == 0)
    def _():
        half = NY // 2
        places = (
            (own, 0, NY),
            (after, NY, NY),
            (oppa, 2 * NY, half),
            (oppb, 2 * NY + half, half),
            (before, 3 * NY, NY),
        )
        copies = [
            pltpu.make_async_copy(src, held.at[pl.ds(at, n)], sems.at[i])
            for i, (src, at, n) in enumerate(places)
        ]
        for copy in copies:
            copy.start()
        for copy in copies:
            copy.wait()

    classes = out_ref.shape[1]
    lanes = lax.broadcasted_iota(jnp.int32, (classes, 128), 1) // QB
    for group in range(NBLK // 4):
        total = None
        for k in range(NT):
            weights = jnp.concatenate(
                [
                    w_ref[c, pl.ds((4 * group + b) * ROWS_C, ROWS_C), pl.ds(k * TILE, TILE)]
                    for b in range(4)
                    for c in range(NC)
                ],
                axis=0,
            )
            labels = jnp.concatenate(
                [held[index_ref[y * PER + (4 * group + b) * NT + k]] for b in range(4)], axis=0
            )
            sums = lax.dot_general(
                labels, weights, (((1,), (1,)), ((), ())), preferred_element_type=F32
            )
            total = sums if total is None else total + sums
        picked = total[:classes]
        for b in range(1, 4):
            picked = jnp.where(lanes == b, total[b * classes : (b + 1) * classes], picked)
        at = pl.ds(128 * group, 128)
        prior = prior_ref[0, :, at].astype(F32)
        out_ref[0, :, at] = (picked + (1.0 - ALPHA) * prior).astype(BF)


def sweep(index, weights, prior, pieces):
    ny, classes, rows = prior.shape
    return pl.pallas_call(
        sweep_kernel,
        grid_spec=pltpu.PrefetchScalarGridSpec(
            num_scalar_prefetch=1,
            grid=(ny,),
            in_specs=[
                pl.BlockSpec((NC,) + weights.shape[1:], lambda y, _: (y, 0, 0)),
                pl.BlockSpec((1, classes, rows), lambda y, _: (y, 0, 0)),
            ]
            + [pl.BlockSpec(memory_space=pl.ANY)] * len(pieces),
            out_specs=pl.BlockSpec((1, classes, rows), lambda y, _: (y, 0, 0)),
            scratch_shapes=[
                pltpu.VMEM((TILES, classes, rows), BF),
                pltpu.SemaphoreType.DMA((len(pieces),)),
            ],
        ),
        out_shape=jax.ShapeDtypeStruct(prior.shape, BF),
        compiler_params=pltpu.CompilerParams(vmem_limit_bytes=48 << 20),
        cost_estimate=pl.CostEstimate(
            flops=2 * ny * rows * NT * TILE * classes * 4,
            bytes_accessed=weights.size * 2 + 4 * prior.size * 2,
            transcendentals=0,
        ),
    )(index, weights, prior, *pieces)


def around_x(mine, beside=lambda *near: near):
    forward = [(i, (i + 1) % NX) for i in range(NX)]
    backward = [(i, (i - 1) % NX) for i in range(NX)]
    before, after = beside(lax.ppermute(mine, "x", forward), lax.ppermute(mine, "x", backward))
    half = NY // 2
    oppa = lax.ppermute(before[:half], "x", forward)
    oppb = lax.ppermute(after[half:], "x", backward)
    return mine, after, oppa, oppb, before


def split_terms(value):
    terms = []
    for scale in (0.99, 1.0, 1.0):
        term = (value * scale).astype(BF)
        value = value - term.astype(F32)
        terms.append(term)
    return terms


def on_device(features, class_bias, logits, tile_lists, valid_counts):
    width = features.shape[1]
    rows, classes = logits.shape
    x, y = lax.axis_index("x"), lax.axis_index("y")
    z, core = lax.axis_index("z"), lax.axis_index("c")

    owners = tile_lists.reshape(PER)
    order = jnp.arange(PER, dtype=jnp.int32)
    same = (owners[:, None] == owners[None, :]) & (order[None, :] < order[:, None])
    position = owners * 2 + jnp.sum(same.astype(jnp.int32), axis=1)
    hits = position.reshape(NBLK, NT)[:, :, None] == jnp.arange(SLOTS, dtype=jnp.int32)
    hits = hits.astype(BF)

    row = core * ROWS_C + z * SUB
    mine = lax.dynamic_slice_in_dim(features.reshape(NBLK, QB, width), row, SUB, axis=1)
    outgoing = jnp.einsum(
        "bs,bf->sf",
        hits.sum(axis=1),
        mine.reshape(NBLK, SUB * width),
        preferred_element_type=F32,
    ).astype(BF)
    arrived = lax.all_to_all(
        outgoing.reshape(TILES, 2 * SUB, width), ("x", "y"), 0, 0, tiled=True
    )

    memory = unitnorm_rows(features)
    queries = unitnorm_rows(arrived.reshape(SLOTS * SUB, width))
    scores = lax.dot_general(
        queries, memory, (((1,), (1,)), ((), ())), preferred_element_type=F32
    ) / SOFTMAX_TEMPER
    columns = jnp.arange(TILE, dtype=jnp.int32)
    scored = jnp.where(columns < valid_counts[0], jnp.exp(scores), 0.0).astype(BF)
    back = lax.all_to_all(
        scored.reshape(TILES, 2 * SUB, TILE), ("x", "y"), 0, 0, tiled=True
    ).reshape(SLOTS, SUB * TILE)
    chosen = jnp.einsum("bks,sf->bkf", hits, back, preferred_element_type=F32)
    chosen = chosen.reshape(NBLK, NT, SUB, TILE)
    denominator = jnp.sum(chosen, axis=(1, 3), keepdims=True)
    scaled = (ALPHA * chosen / denominator).astype(BF)
    scaled = scaled.transpose(0, 2, 1, 3).reshape(NBLK, SUB, NT * TILE)

    part = jnp.sum(jnp.exp(logits.astype(F32) + class_bias[None, :]), axis=1)
    high, middle, low = split_terms(part)
    terms = jnp.concatenate([high, middle, low, jnp.zeros_like(low)])
    piece = jnp.concatenate([scaled, terms.reshape(1, SUB, NT * TILE)])
    over_z = lax.all_to_all(
        jnp.broadcast_to(piece, (NZ,) + piece.shape), "z", 0, 0, tiled=True
    )

    piece = over_z[:, :NBLK].transpose(1, 0, 2, 3).reshape(NBLK * ROWS_C, NT * TILE)
    weights = lax.all_gather(piece, ("y", "c"), axis=0, tiled=False)

    terms = jnp.sum(over_z[:, NBLK].astype(F32), axis=0).reshape(4, rows)
    totals = terms[0] + terms[1] + terms[2]
    raw, _ = lax.optimization_barrier((logits, over_z))
    raw = lax.all_to_all(
        raw.T.reshape(NY, classes // NY, rows), "y", 0, 0, tiled=True
    )
    totals = totals + lax.ppermute(totals, "c", [(0, 1), (1, 0)])
    known = jnp.concatenate([totals, owners.astype(F32), jnp.zeros((128 - PER,), F32)])
    known, _ = lax.optimization_barrier((known, raw))
    known = lax.all_to_all(
        jnp.broadcast_to(known, (TILES,) + known.shape), ("x", "y"), 0, 0, tiled=True
    )
    raw = around_x(raw, lambda *near: lax.optimization_barrier((*near, known))[:2])
    known = known.reshape(NX, NY, -1)
    known = lax.dynamic_slice_in_dim(jnp.concatenate([known, known]), x, NX, axis=0)
    totals = known[:, :, :rows]

    bias = lax.dynamic_slice_in_dim(class_bias.reshape(NY, classes // NY), y, 1, axis=0)
    bias = bias.reshape(1, classes // NY, 1)
    half = NY // 2
    sums = totals[0], totals[1], totals[2, :half], totals[2, half:], totals[3]
    priors = tuple(
        (jnp.exp(r.astype(F32) + bias) / t[:, None, :]).astype(BF) for r, t in zip(raw, sums)
    )

    named = known[0, :, rows : rows + PER].astype(jnp.int32).reshape(NY * PER)
    index = (named // NY - x) % NX * NY + named % NY

    labels = sweep(index, weights, priors[0], priors)
    spread = sweep(index, weights, priors[0], around_x(labels))
    spread = lax.all_to_all(spread, "y", 0, 0, tiled=True)
    return jnp.log(spread.reshape(classes, rows).T.astype(F32))


def solution(mesh):
    split = Mesh(mesh.devices.reshape(NX, NY, NZ, NC), ("x", "y", "z", "c"))
    dp, tensor = ("x", "y"), ("z", "c")
    in_specs = (P(dp, None), P(tensor), P(dp, tensor), P(dp, None), P(dp))
    return jax.shard_map(
        on_device, mesh=split, in_specs=in_specs, out_specs=P(dp, tensor), check_vma=False
    )
```

```python
import math

import jax
import jax.numpy as jnp
from jax import lax
from jax.experimental import pallas as pl
from jax.experimental.pallas import tpu as pltpu
from jax.sharding import Mesh
from jax.sharding import PartitionSpec as P

ALPHA = 0.75
SOFTMAX_TEMPER = 0.05
EPSILON = 1e-06

NX, NY, NZ, NC = 4, 8, 8, 2
TILES = NX * NY
TILE = 512
QB = 32
NBLK = 16
NT = 2
PER = NBLK * NT
SLOTS = TILES * 2
SUB = 2
ROWS_C = QB // NC
BF = jnp.bfloat16
F32 = jnp.float32


def unitnorm_rows(features):
    wide = features.astype(F32)
    scale = lax.rsqrt(jnp.mean(wide * wide, axis=-1, keepdims=True) + EPSILON)
    return (wide * scale / math.sqrt(wide.shape[-1])).astype(BF)


GROUPS = (((0, 0), (1, 1), (2, 7)), ((0, 2), (1, 6)), ((0, 3), (1, 5), (2, 4)))


def sweep_kernel(index_ref, prior_ref, *refs):
    weights, (own, after, oppa, oppb, before), refs = refs[:6], refs[6:11], refs[11:]
    out_ref, held, kept, sems, weight_sems = refs
    step = pl.program_id(0)
    y = lax.rem(index_ref[NY * PER + 1] - step + NY, NY)
    size = NBLK * ROWS_C
    brought = {
        (side, back): pltpu.make_async_copy(
            weights[3 * side + group].at[pl.ds(place * size, size)],
            kept.at[side, back],
            weight_sems.at[side, back],
        )
        for side in range(NC)
        for group, places in enumerate(GROUPS)
        for place, back in places
    }

    @pl.when(step == 0)
    def _():
        half = NY // 2
        places = (
            (own, 0, NY),
            (after, NY, NY),
            (oppa, 2 * NY, half),
            (oppb, 2 * NY + half, half),
            (before, 3 * NY, NY),
        )
        copies = [
            pltpu.make_async_copy(src, held.at[pl.ds(at, n)], sems.at[i])
            for i, (src, at, n) in enumerate(places)
        ]
        for copy in copies:
            copy.start()
        for back in range(NY):
            for side in range(NC):
                brought[side, back].start()
        for copy in copies:
            copy.wait()

    for back in range(NY):

        @pl.when(step == back)
        def _():
            for side in range(NC):
                brought[side, back].wait()

    first_core = index_ref[NY * PER] == 0
    classes = out_ref.shape[1]
    lanes = lax.broadcasted_iota(jnp.int32, (classes, 128), 1) // QB
    for group in range(NBLK // 4):
        total = None
        for k in range(NT):
            rows = []
            for b in range(4):
                at = pl.ds((4 * group + b) * ROWS_C, ROWS_C), pl.ds(k * TILE, TILE)
                mine, other = kept[0, step, *at], kept[1, step, *at]
                rows.append(jnp.where(first_core, mine, other))
                rows.append(jnp.where(first_core, other, mine))
            labels = jnp.concatenate(
                [held[index_ref[y * PER + (4 * group + b) * NT + k]] for b in range(4)], axis=0
            )
            sums = lax.dot_general(
                labels,
                jnp.concatenate(rows, axis=0),
                (((1,), (1,)), ((), ())),
                preferred_element_type=F32,
            )
            total = sums if total is None else total + sums
        picked = total[:classes]
        for b in range(1, 4):
            picked = jnp.where(lanes == b, total[b * classes : (b + 1) * classes], picked)
        at = pl.ds(128 * group, 128)
        prior = prior_ref[0, :, at].astype(F32)
        out_ref[0, :, at] = (picked + (1.0 - ALPHA) * prior).astype(BF)


def sweep(index, weights, prior, pieces):
    ny, classes, rows = prior.shape

    def by_y(step, index):
        return lax.rem(index[NY * PER + 1] - step + NY, NY), 0, 0

    return pl.pallas_call(
        sweep_kernel,
        grid_spec=pltpu.PrefetchScalarGridSpec(
            num_scalar_prefetch=1,
            grid=(ny,),
            in_specs=[pl.BlockSpec((1, classes, rows), by_y)]
            + [pl.BlockSpec(memory_space=pl.ANY)] * (len(weights) + len(pieces)),
            out_specs=pl.BlockSpec((1, classes, rows), by_y),
            scratch_shapes=[
                pltpu.VMEM((TILES, classes, rows), BF),
                pltpu.VMEM((NC, NY, NBLK * ROWS_C, NT * TILE), BF),
                pltpu.SemaphoreType.DMA((len(pieces),)),
                pltpu.SemaphoreType.DMA((NC, NY)),
            ],
        ),
        out_shape=jax.ShapeDtypeStruct(prior.shape, BF),
        compiler_params=pltpu.CompilerParams(vmem_limit_bytes=32 << 20),
        cost_estimate=pl.CostEstimate(
            flops=2 * ny * rows * NT * TILE * classes * 4,
            bytes_accessed=ny * rows * NT * TILE * 2 + 4 * prior.size * 2,
            transcendentals=0,
        ),
    )(index, prior, *weights, *pieces)


def around_y(mine):
    forward = [(i, (i + 1) % NY) for i in range(NY)]
    backward = [(i, (i - 1) % NY) for i in range(NY)]
    before, after = [mine], [mine]
    for _ in range(3):
        before.append(lax.ppermute(before[-1], "y", forward))
        after.append(lax.ppermute(after[-1], "y", backward))
    half = mine.shape[0] // 2
    far = (
        lax.ppermute(before[3][:half], "y", forward),
        lax.ppermute(after[3][half:], "y", backward),
    )
    groups = (
        jnp.concatenate([mine, before[1], after[1]]),
        jnp.concatenate([before[2], after[2]]),
        jnp.concatenate([before[3], after[3], *far]),
    )
    return groups + tuple(lax.ppermute(g, "c", [(0, 1), (1, 0)]) for g in groups)


def around_x(mine, beside=lambda *near: near):
    forward = [(i, (i + 1) % NX) for i in range(NX)]
    backward = [(i, (i - 1) % NX) for i in range(NX)]
    before, after = beside(lax.ppermute(mine, "x", forward), lax.ppermute(mine, "x", backward))
    half = NY // 2
    oppa = lax.ppermute(before[:half], "x", forward)
    oppb = lax.ppermute(after[half:], "x", backward)
    return mine, after, oppa, oppb, before


def split_terms(value):
    terms = []
    for scale in (0.99, 1.0, 1.0):
        term = (value * scale).astype(BF)
        value = value - term.astype(F32)
        terms.append(term)
    return terms


def on_device(features, class_bias, logits, tile_lists, valid_counts):
    width = features.shape[1]
    rows, classes = logits.shape
    x, y = lax.axis_index("x"), lax.axis_index("y")
    z, core = lax.axis_index("z"), lax.axis_index("c")

    owners = tile_lists.reshape(PER)
    order = jnp.arange(PER, dtype=jnp.int32)
    same = (owners[:, None] == owners[None, :]) & (order[None, :] < order[:, None])
    position = owners * 2 + jnp.sum(same.astype(jnp.int32), axis=1)
    hits = position.reshape(NBLK, NT)[:, :, None] == jnp.arange(SLOTS, dtype=jnp.int32)
    hits = hits.astype(BF)

    row = core * ROWS_C + z * SUB
    mine = lax.dynamic_slice_in_dim(features.reshape(NBLK, QB, width), row, SUB, axis=1)
    outgoing = jnp.einsum(
        "bs,bf->sf",
        hits.sum(axis=1),
        mine.reshape(NBLK, SUB * width),
        preferred_element_type=F32,
    ).astype(BF)
    arrived = lax.all_to_all(
        outgoing.reshape(TILES, 2 * SUB, width), ("x", "y"), 0, 0, tiled=True
    )

    memory = unitnorm_rows(features)
    queries = unitnorm_rows(arrived.reshape(SLOTS * SUB, width))
    scores = lax.dot_general(
        queries, memory, (((1,), (1,)), ((), ())), preferred_element_type=F32
    ) / SOFTMAX_TEMPER
    columns = jnp.arange(TILE, dtype=jnp.int32)
    scored = jnp.where(columns < valid_counts[0], jnp.exp(scores), 0.0).astype(BF)
    back = lax.all_to_all(
        scored.reshape(TILES, 2 * SUB, TILE), ("x", "y"), 0, 0, tiled=True
    ).reshape(SLOTS, SUB * TILE)
    chosen = jnp.einsum("bks,sf->bkf", hits, back, preferred_element_type=F32)
    chosen = chosen.reshape(NBLK, NT, SUB, TILE)
    denominator = jnp.sum(chosen, axis=(1, 3), keepdims=True)
    scaled = (ALPHA * chosen / denominator).astype(BF)
    scaled = scaled.transpose(0, 2, 1, 3).reshape(NBLK, SUB, NT * TILE)

    part = jnp.sum(jnp.exp(logits.astype(F32) + class_bias[None, :]), axis=1)
    high, middle, low = split_terms(part)
    terms = jnp.concatenate([high, middle, low, jnp.zeros_like(low)])
    piece = jnp.concatenate([scaled, terms.reshape(1, SUB, NT * TILE)])
    over_z = lax.all_to_all(
        jnp.broadcast_to(piece, (NZ,) + piece.shape), "z", 0, 0, tiled=True
    )

    piece = over_z[:, :NBLK].transpose(1, 0, 2, 3).reshape(NBLK * ROWS_C, NT * TILE)
    weights = around_y(piece)

    terms = jnp.sum(over_z[:, NBLK].astype(F32), axis=0).reshape(4, rows)
    totals = terms[0] + terms[1] + terms[2]
    raw, _ = lax.optimization_barrier((logits, over_z))
    raw = lax.all_to_all(
        raw.T.reshape(NY, classes // NY, rows), "y", 0, 0, tiled=True
    )
    totals = totals + lax.ppermute(totals, "c", [(0, 1), (1, 0)])
    known = jnp.concatenate([totals, owners.astype(F32), jnp.zeros((128 - PER,), F32)])
    known, _ = lax.optimization_barrier((known, raw))
    known = lax.all_to_all(
        jnp.broadcast_to(known, (TILES,) + known.shape), ("x", "y"), 0, 0, tiled=True
    )
    raw = around_x(raw, lambda *near: lax.optimization_barrier((*near, known))[:2])
    known = known.reshape(NX, NY, -1)
    known = lax.dynamic_slice_in_dim(jnp.concatenate([known, known]), x, NX, axis=0)
    totals = known[:, :, :rows]

    bias = lax.dynamic_slice_in_dim(class_bias.reshape(NY, classes // NY), y, 1, axis=0)
    bias = bias.reshape(1, classes // NY, 1)
    half = NY // 2
    sums = totals[0], totals[1], totals[2, :half], totals[2, half:], totals[3]
    priors = tuple(
        (jnp.exp(r.astype(F32) + bias) / t[:, None, :]).astype(BF) for r, t in zip(raw, sums)
    )

    named = known[0, :, rows : rows + PER].astype(jnp.int32).reshape(NY * PER)
    index = (named // NY - x) % NX * NY + named % NY

    index = jnp.concatenate([index, core.reshape(1), y.reshape(1)])

    labels = sweep(index, weights, priors[0], priors)
    spread = sweep(index, weights, priors[0], around_x(labels))
    spread = lax.all_to_all(spread, "y", 0, 0, tiled=True)
    return jnp.log(spread.reshape(classes, rows).T.astype(F32))


def solution(mesh):
    split = Mesh(mesh.devices.reshape(NX, NY, NZ, NC), ("x", "y", "z", "c"))
    dp, tensor = ("x", "y"), ("z", "c")
    in_specs = (P(dp, None), P(tensor), P(dp, tensor), P(dp, None), P(dp))
    return jax.shard_map(
        on_device, mesh=split, in_specs=in_specs, out_specs=P(dp, tensor), check_vma=False
    )
```

```python
import math

import jax
import jax.numpy as jnp
from jax import lax
from jax.experimental import pallas as pl
from jax.experimental.pallas import tpu as pltpu
from jax.sharding import Mesh
from jax.sharding import PartitionSpec as P

ALPHA = 0.75
SOFTMAX_TEMPER = 0.05
EPSILON = 1e-06

NX, NY, NZ, NC = 4, 8, 8, 2
TILES = NX * NY
TILE = 512
QB = 32
NBLK = 16
NT = 2
PER = NBLK * NT
SLOTS = TILES * 2
SUB = 2
ROWS_C = QB // NC
BF = jnp.bfloat16
F32 = jnp.float32


def unitnorm_rows(features):
    wide = features.astype(F32)
    scale = lax.rsqrt(jnp.mean(wide * wide, axis=-1, keepdims=True) + EPSILON)
    return (wide * scale / math.sqrt(wide.shape[-1])).astype(BF)


def sweep_kernel(index_ref, w_ref, prior_ref, own, after, oppa, oppb, before, out_ref, held, sems):
    y = pl.program_id(0)

    @pl.when(y == 0)
    def _():
        half = NY // 2
        places = (
            (own, 0, NY),
            (after, NY, NY),
            (oppa, 2 * NY, half),
            (oppb, 2 * NY + half, half),
            (before, 3 * NY, NY),
        )
        copies = [
            pltpu.make_async_copy(src, held.at[pl.ds(at, n)], sems.at[i])
            for i, (src, at, n) in enumerate(places)
        ]
        for copy in copies:
            copy.start()
        for copy in copies:
            copy.wait()

    classes = out_ref.shape[1]
    lanes = lax.broadcasted_iota(jnp.int32, (classes, 128), 1) // QB
    for group in range(NBLK // 4):
        total = None
        for k in range(NT):
            weights = jnp.concatenate(
                [
                    w_ref[c, pl.ds((4 * group + b) * ROWS_C, ROWS_C), pl.ds(k * TILE, TILE)]
                    for b in range(4)
                    for c in range(NC)
                ],
                axis=0,
            )
            labels = jnp.concatenate(
                [held[index_ref[y * PER + (4 * group + b) * NT + k]] for b in range(4)], axis=0
            )
            sums = lax.dot_general(
                labels, weights, (((1,), (1,)), ((), ())), preferred_element_type=F32
            )
            total = sums if total is None else total + sums
        picked = total[:classes]
        for b in range(1, 4):
            picked = jnp.where(lanes == b, total[b * classes : (b + 1) * classes], picked)
        at = pl.ds(128 * group, 128)
        prior = prior_ref[0, :, at].astype(F32)
        out_ref[0, :, at] = (picked + (1.0 - ALPHA) * prior).astype(BF)


def sweep(index, weights, prior, pieces, grant):
    ny, classes, rows = prior.shape
    return pl.pallas_call(
        sweep_kernel,
        grid_spec=pltpu.PrefetchScalarGridSpec(
            num_scalar_prefetch=1,
            grid=(ny,),
            in_specs=[
                pl.BlockSpec((NC,) + weights.shape[1:], lambda y, _: (y, 0, 0)),
                pl.BlockSpec((1, classes, rows), lambda y, _: (y, 0, 0)),
            ]
            + [pl.BlockSpec(memory_space=pl.ANY)] * len(pieces),
            out_specs=pl.BlockSpec((1, classes, rows), lambda y, _: (y, 0, 0)),
            scratch_shapes=[
                pltpu.VMEM((TILES, classes, rows), BF),
                pltpu.SemaphoreType.DMA((len(pieces),)),
            ],
        ),
        out_shape=jax.ShapeDtypeStruct(prior.shape, BF),
        compiler_params=pltpu.CompilerParams(vmem_limit_bytes=grant << 20),
        cost_estimate=pl.CostEstimate(
            flops=2 * ny * rows * NT * TILE * classes * 4,
            bytes_accessed=weights.size * 2 + 4 * prior.size * 2,
            transcendentals=0,
        ),
    )(index, weights, prior, *pieces)


def around_x(mine):
    forward = [(i, (i + 1) % NX) for i in range(NX)]
    backward = [(i, (i - 1) % NX) for i in range(NX)]
    before = lax.ppermute(mine, "x", forward)
    after = lax.ppermute(mine, "x", backward)
    half = NY // 2
    oppa = lax.ppermute(before[:half], "x", forward)
    oppb = lax.ppermute(after[half:], "x", backward)
    return mine, after, oppa, oppb, before


def split_terms(value):
    terms = []
    for scale in (0.99, 1.0, 1.0):
        term = (value * scale).astype(BF)
        value = value - term.astype(F32)
        terms.append(term)
    return terms


def on_device(features, class_bias, logits, tile_lists, valid_counts):
    width = features.shape[1]
    rows, classes = logits.shape
    x, y = lax.axis_index("x"), lax.axis_index("y")
    z, core = lax.axis_index("z"), lax.axis_index("c")

    owners = tile_lists.reshape(PER)
    order = jnp.arange(PER, dtype=jnp.int32)
    same = (owners[:, None] == owners[None, :]) & (order[None, :] < order[:, None])
    position = owners * 2 + jnp.sum(same.astype(jnp.int32), axis=1)
    hits = position.reshape(NBLK, NT)[:, :, None] == jnp.arange(SLOTS, dtype=jnp.int32)
    hits = hits.astype(BF)

    row = core * ROWS_C + z * SUB
    mine = lax.dynamic_slice_in_dim(features.reshape(NBLK, QB, width), row, SUB, axis=1)
    outgoing = jnp.einsum(
        "bs,bf->sf",
        hits.sum(axis=1),
        mine.reshape(NBLK, SUB * width),
        preferred_element_type=F32,
    ).astype(BF)
    arrived = lax.all_to_all(
        outgoing.reshape(TILES, 2 * SUB, width), ("x", "y"), 0, 0, tiled=True
    )

    memory = unitnorm_rows(features)
    queries = unitnorm_rows(arrived.reshape(SLOTS * SUB, width))
    scores = lax.dot_general(
        queries, memory, (((1,), (1,)), ((), ())), preferred_element_type=F32
    ) / SOFTMAX_TEMPER
    columns = jnp.arange(TILE, dtype=jnp.int32)
    scored = jnp.where(columns < valid_counts[0], jnp.exp(scores), 0.0).astype(BF)
    back = lax.all_to_all(
        scored.reshape(TILES, 2 * SUB, TILE), ("x", "y"), 0, 0, tiled=True
    ).reshape(SLOTS, SUB * TILE)
    chosen = jnp.einsum("bks,sf->bkf", hits, back, preferred_element_type=F32)
    chosen = chosen.reshape(NBLK, NT, SUB, TILE)
    denominator = jnp.sum(chosen, axis=(1, 3), keepdims=True)
    scaled = (ALPHA * chosen / denominator).astype(BF)
    scaled = scaled.transpose(0, 2, 1, 3).reshape(NBLK, SUB, NT * TILE)

    part = jnp.sum(jnp.exp(logits.astype(F32) + class_bias[None, :]), axis=1)
    high, middle, low = split_terms(part)
    terms = jnp.concatenate([high, middle, low, jnp.zeros_like(low)])
    piece = jnp.concatenate([scaled, terms.reshape(1, SUB, NT * TILE)])
    over_z = lax.all_to_all(
        jnp.broadcast_to(piece, (NZ,) + piece.shape), "z", 0, 0, tiled=True
    )

    piece = over_z[:, :NBLK].transpose(1, 0, 2, 3).reshape(NBLK * ROWS_C, NT * TILE)
    weights = lax.all_gather(piece, ("y", "c"), axis=0, tiled=False)

    terms = jnp.sum(over_z[:, NBLK].astype(F32), axis=0).reshape(4, rows)
    totals = terms[0] + terms[1] + terms[2]
    raw, _ = lax.optimization_barrier((logits, over_z))
    raw = lax.all_to_all(
        raw.T.reshape(NY, classes // NY, rows), "y", 0, 0, tiled=True
    )
    totals = totals + lax.ppermute(totals, "c", [(0, 1), (1, 0)])
    known = jnp.concatenate([totals, owners.astype(F32), jnp.zeros((128 - PER,), F32)])
    known, _ = lax.optimization_barrier((known, raw))
    known = lax.all_to_all(
        jnp.broadcast_to(known, (TILES,) + known.shape), ("x", "y"), 0, 0, tiled=True
    )
    raw = around_x(raw)
    known = known.reshape(NX, NY, -1)
    known = lax.dynamic_slice_in_dim(jnp.concatenate([known, known]), x, NX, axis=0)
    totals = known[:, :, :rows]

    bias = lax.dynamic_slice_in_dim(class_bias.reshape(NY, classes // NY), y, 1, axis=0)
    bias = bias.reshape(1, classes // NY, 1)
    half = NY // 2
    sums = totals[0], totals[1], totals[2, :half], totals[2, half:], totals[3]
    priors = tuple(
        (jnp.exp(r.astype(F32) + bias) / t[:, None, :]).astype(BF) for r, t in zip(raw, sums)
    )

    named = known[0, :, rows : rows + PER].astype(jnp.int32).reshape(NY * PER)
    index = (named // NY - x) % NX * NY + named % NY

    labels = sweep(index, weights, priors[0], priors, 48)
    spread = sweep(index, weights, priors[0], around_x(labels), 16)
    spread = lax.all_to_all(spread, "y", 0, 0, tiled=True)
    return jnp.log(spread.reshape(classes, rows).T.astype(F32))


def solution(mesh):
    split = Mesh(mesh.devices.reshape(NX, NY, NZ, NC), ("x", "y", "z", "c"))
    dp, tensor = ("x", "y"), ("z", "c")
    in_specs = (P(dp, None), P(tensor), P(dp, tensor), P(dp, None), P(dp))
    return jax.shard_map(
        on_device, mesh=split, in_specs=in_specs, out_specs=P(dp, tensor), check_vma=False
    )
```

```python
import math

import jax
import jax.numpy as jnp
from jax import lax
from jax.experimental import pallas as pl
from jax.experimental.pallas import tpu as pltpu
from jax.sharding import Mesh
from jax.sharding import PartitionSpec as P

ALPHA = 0.75
SOFTMAX_TEMPER = 0.05
EPSILON = 1e-06

NX, NY, NZ, NC = 4, 8, 8, 2
TILES = NX * NY
TILE = 512
QB = 32
NBLK = 16
NT = 2
PER = NBLK * NT
SLOTS = TILES * 2
SUB = 2
ROWS_C = QB // NC
BF = jnp.bfloat16
F32 = jnp.float32


def unitnorm_rows(features):
    wide = features.astype(F32)
    scale = lax.rsqrt(jnp.mean(wide * wide, axis=-1, keepdims=True) + EPSILON)
    return (wide * scale / math.sqrt(wide.shape[-1])).astype(BF)


def sweep_kernel(index_ref, w_ref, prior_ref, own, after, oppa, oppb, before, out_ref, held, sems):
    y = pl.program_id(0)

    @pl.when(y == 0)
    def _():
        half = NY // 2
        places = (
            (own, 0, NY),
            (after, NY, NY),
            (oppa, 2 * NY, half),
            (oppb, 2 * NY + half, half),
            (before, 3 * NY, NY),
        )
        copies = [
            pltpu.make_async_copy(src, held.at[pl.ds(at, n)], sems.at[i])
            for i, (src, at, n) in enumerate(places)
        ]
        for copy in copies:
            copy.start()
        for copy in copies:
            copy.wait()

    classes = out_ref.shape[1]
    lanes = lax.broadcasted_iota(jnp.int32, (classes, 128), 1) // QB
    for group in range(NBLK // 4):
        total = None
        for k in range(NT):
            weights = jnp.concatenate(
                [
                    w_ref[c, pl.ds((4 * group + b) * ROWS_C, ROWS_C), pl.ds(k * TILE, TILE)]
                    for b in range(4)
                    for c in range(NC)
                ],
                axis=0,
            )
            labels = jnp.concatenate(
                [held[index_ref[y * PER + (4 * group + b) * NT + k]] for b in range(4)], axis=0
            )
            sums = lax.dot_general(
                labels, weights, (((1,), (1,)), ((), ())), preferred_element_type=F32
            )
            total = sums if total is None else total + sums
        picked = total[:classes]
        for b in range(1, 4):
            picked = jnp.where(lanes == b, total[b * classes : (b + 1) * classes], picked)
        at = pl.ds(128 * group, 128)
        prior = prior_ref[0, :, at].astype(F32)
        out_ref[0, :, at] = (picked + (1.0 - ALPHA) * prior).astype(BF)


def sweep(index, weights, prior, pieces, grant):
    ny, classes, rows = prior.shape
    return pl.pallas_call(
        sweep_kernel,
        grid_spec=pltpu.PrefetchScalarGridSpec(
            num_scalar_prefetch=1,
            grid=(ny,),
            in_specs=[
                pl.BlockSpec((NC,) + weights.shape[1:], lambda y, _: (y, 0, 0)),
                pl.BlockSpec((1, classes, rows), lambda y, _: (y, 0, 0)),
            ]
            + [pl.BlockSpec(memory_space=pl.ANY)] * len(pieces),
            out_specs=pl.BlockSpec((1, classes, rows), lambda y, _: (y, 0, 0)),
            scratch_shapes=[
                pltpu.VMEM((TILES, classes, rows), BF),
                pltpu.SemaphoreType.DMA((len(pieces),)),
            ],
        ),
        out_shape=jax.ShapeDtypeStruct(prior.shape, BF),
        compiler_params=pltpu.CompilerParams(vmem_limit_bytes=grant << 20),
        cost_estimate=pl.CostEstimate(
            flops=2 * ny * rows * NT * TILE * classes * 4,
            bytes_accessed=weights.size * 2 + 4 * prior.size * 2,
            transcendentals=0,
        ),
    )(index, weights, prior, *pieces)


def around_x(mine):
    forward = [(i, (i + 1) % NX) for i in range(NX)]
    backward = [(i, (i - 1) % NX) for i in range(NX)]
    before = lax.ppermute(mine, "x", forward)
    after = lax.ppermute(mine, "x", backward)
    half = NY // 2
    oppa = lax.ppermute(before[:half], "x", forward)
    oppb = lax.ppermute(after[half:], "x", backward)
    return mine, after, oppa, oppb, before


def split_terms(value):
    terms = []
    for scale in (0.99, 1.0, 1.0):
        term = (value * scale).astype(BF)
        value = value - term.astype(F32)
        terms.append(term)
    return terms


def on_device(features, class_bias, logits, tile_lists, valid_counts):
    width = features.shape[1]
    rows, classes = logits.shape
    x, y = lax.axis_index("x"), lax.axis_index("y")
    z, core = lax.axis_index("z"), lax.axis_index("c")

    owners = tile_lists.reshape(PER)
    order = jnp.arange(PER, dtype=jnp.int32)
    same = (owners[:, None] == owners[None, :]) & (order[None, :] < order[:, None])
    position = owners * 2 + jnp.sum(same.astype(jnp.int32), axis=1)
    hits = position.reshape(NBLK, NT)[:, :, None] == jnp.arange(SLOTS, dtype=jnp.int32)
    hits = hits.astype(BF)

    row = core * ROWS_C + z * SUB
    mine = lax.dynamic_slice_in_dim(features.reshape(NBLK, QB, width), row, SUB, axis=1)
    outgoing = jnp.einsum(
        "bs,bf->sf",
        hits.sum(axis=1),
        mine.reshape(NBLK, SUB * width),
        preferred_element_type=F32,
    ).astype(BF)
    arrived = lax.all_to_all(
        outgoing.reshape(TILES, 2 * SUB, width), ("x", "y"), 0, 0, tiled=True
    )

    memory = unitnorm_rows(features)
    queries = unitnorm_rows(arrived.reshape(SLOTS * SUB, width))
    scores = lax.dot_general(
        queries, memory, (((1,), (1,)), ((), ())), preferred_element_type=F32
    ) / SOFTMAX_TEMPER
    columns = jnp.arange(TILE, dtype=jnp.int32)
    scored = jnp.where(columns < valid_counts[0], jnp.exp(scores), 0.0).astype(BF)
    back = lax.all_to_all(
        scored.reshape(TILES, 2 * SUB, TILE), ("x", "y"), 0, 0, tiled=True
    ).reshape(SLOTS, SUB * TILE)
    chosen = jnp.einsum("bks,sf->bkf", hits, back, preferred_element_type=F32)
    chosen = chosen.reshape(NBLK, NT, SUB, TILE)
    denominator = jnp.sum(chosen, axis=(1, 3), keepdims=True)
    scaled = (ALPHA * chosen / denominator).astype(BF)
    scaled = scaled.transpose(0, 2, 1, 3).reshape(NBLK, SUB, NT * TILE)

    part = jnp.sum(jnp.exp(logits.astype(F32) + class_bias[None, :]), axis=1)
    part = part + lax.ppermute(part, "c", [(0, 1), (1, 0)])
    high, middle, low = split_terms(part)
    terms = jnp.concatenate([high, middle, low, jnp.zeros_like(low)])
    piece = jnp.concatenate([scaled, terms.reshape(1, SUB, NT * TILE)])
    over_z = lax.all_to_all(
        jnp.broadcast_to(piece, (NZ,) + piece.shape), "z", 0, 0, tiled=True
    )

    piece = over_z[:, :NBLK].transpose(1, 0, 2, 3).reshape(NBLK * ROWS_C, NT * TILE)
    names = jnp.zeros((16, NT * TILE), BF).at[0, :PER].set(owners.astype(BF))
    piece = jnp.concatenate([piece, names])
    weights = lax.all_gather(piece, ("y", "c"), axis=0, tiled=False)

    terms = jnp.sum(over_z[:, NBLK].astype(F32), axis=0).reshape(4, rows)
    totals = terms[0] + terms[1] + terms[2]
    adjusted = logits.astype(F32) + class_bias[None, :]
    prior = (jnp.exp(adjusted) / totals[:, None]).astype(BF)
    prior = lax.all_to_all(
        prior.T.reshape(NY, classes // NY, rows), "y", 0, 0, tiled=True
    )
    priors = around_x(prior)

    named = weights[::NC, NBLK * ROWS_C, :PER].astype(jnp.int32).reshape(NY * PER)
    index = (named // NY - x) % NX * NY + named % NY

    labels = sweep(index, weights, priors[0], priors, 48)
    spread = sweep(index, weights, priors[0], around_x(labels), 16)
    spread = lax.all_to_all(spread, "y", 0, 0, tiled=True)
    return jnp.log(spread.reshape(classes, rows).T.astype(F32))


def solution(mesh):
    split = Mesh(mesh.devices.reshape(NX, NY, NZ, NC), ("x", "y", "z", "c"))
    dp, tensor = ("x", "y"), ("z", "c")
    in_specs = (P(dp, None), P(tensor), P(dp, tensor), P(dp, None), P(dp))
    return jax.shard_map(
        on_device, mesh=split, in_specs=in_specs, out_specs=P(dp, tensor), check_vma=False
    )
```

```python
import math

import jax
import jax.numpy as jnp
from jax import lax
from jax.experimental import pallas as pl
from jax.experimental.pallas import tpu as pltpu
from jax.sharding import Mesh
from jax.sharding import PartitionSpec as P

ALPHA = 0.75
SOFTMAX_TEMPER = 0.05
EPSILON = 1e-06

NX, NY, NZ, NC = 4, 8, 8, 2
TILES = NX * NY
TILE = 512
QB = 32
NBLK = 16
NT = 2
PER = NBLK * NT
SLOTS = TILES * 2
SUB = 2
ROWS_C = QB // NC
BF = jnp.bfloat16
F32 = jnp.float32


def unitnorm_rows(features):
    wide = features.astype(F32)
    scale = lax.rsqrt(jnp.mean(wide * wide, axis=-1, keepdims=True) + EPSILON)
    return (wide * scale / math.sqrt(wide.shape[-1])).astype(BF)


def sweep_kernel(index_ref, w_ref, prior_ref, own, after, oppa, oppb, before, out_ref, held, sems):
    y = pl.program_id(0)

    @pl.when(y == 0)
    def _():
        half = NY // 2
        places = (
            (own, 0, NY),
            (after, NY, NY),
            (oppa, 2 * NY, half),
            (oppb, 2 * NY + half, half),
            (before, 3 * NY, NY),
        )
        copies = [
            pltpu.make_async_copy(src, held.at[pl.ds(at, n)], sems.at[i])
            for i, (src, at, n) in enumerate(places)
        ]
        for copy in copies:
            copy.start()
        for copy in copies:
            copy.wait()

    classes = out_ref.shape[1]
    lanes = lax.broadcasted_iota(jnp.int32, (classes, 128), 1) // QB
    for group in range(NBLK // 4):
        total = None
        for k in range(NT):
            weights = jnp.concatenate(
                [
                    w_ref[c, pl.ds((4 * group + b) * ROWS_C, ROWS_C), pl.ds(k * TILE, TILE)]
                    for b in range(4)
                    for c in range(NC)
                ],
                axis=0,
            )
            labels = jnp.concatenate(
                [held[index_ref[y * PER + (4 * group + b) * NT + k]] for b in range(4)], axis=0
            )
            sums = lax.dot_general(
                labels, weights, (((1,), (1,)), ((), ())), preferred_element_type=F32
            )
            total = sums if total is None else total + sums
        picked = total[:classes]
        for b in range(1, 4):
            picked = jnp.where(lanes == b, total[b * classes : (b + 1) * classes], picked)
        at = pl.ds(128 * group, 128)
        prior = prior_ref[0, :, at].astype(F32)
        out_ref[0, :, at] = (picked + (1.0 - ALPHA) * prior).astype(BF)


def sweep(index, weights, prior, pieces, grant):
    ny, classes, rows = prior.shape
    return pl.pallas_call(
        sweep_kernel,
        grid_spec=pltpu.PrefetchScalarGridSpec(
            num_scalar_prefetch=1,
            grid=(ny,),
            in_specs=[
                pl.BlockSpec((NC,) + weights.shape[1:], lambda y, _: (y, 0, 0)),
                pl.BlockSpec((1, classes, rows), lambda y, _: (y, 0, 0)),
            ]
            + [pl.BlockSpec(memory_space=pl.ANY)] * len(pieces),
            out_specs=pl.BlockSpec((1, classes, rows), lambda y, _: (y, 0, 0)),
            scratch_shapes=[
                pltpu.VMEM((TILES, classes, rows), BF),
                pltpu.SemaphoreType.DMA((len(pieces),)),
            ],
        ),
        out_shape=jax.ShapeDtypeStruct(prior.shape, BF),
        compiler_params=pltpu.CompilerParams(vmem_limit_bytes=grant << 20),
        cost_estimate=pl.CostEstimate(
            flops=2 * ny * rows * NT * TILE * classes * 4,
            bytes_accessed=weights.size * 2 + 4 * prior.size * 2,
            transcendentals=0,
        ),
    )(index, weights, prior, *pieces)


def around_x(mine):
    forward = [(i, (i + 1) % NX) for i in range(NX)]
    backward = [(i, (i - 1) % NX) for i in range(NX)]
    before = lax.ppermute(mine, "x", forward)
    after = lax.ppermute(mine, "x", backward)
    half = NY // 2
    oppa = lax.ppermute(before[:half], "x", forward)
    oppb = lax.ppermute(after[half:], "x", backward)
    return mine, after, oppa, oppb, before


def split_terms(value):
    terms = []
    for scale in (0.99, 1.0, 1.0):
        term = (value * scale).astype(BF)
        value = value - term.astype(F32)
        terms.append(term)
    return terms


def on_device(features, class_bias, logits, tile_lists, valid_counts):
    width = features.shape[1]
    rows, classes = logits.shape
    x, y = lax.axis_index("x"), lax.axis_index("y")
    z, core = lax.axis_index("z"), lax.axis_index("c")

    owners = tile_lists.reshape(PER)
    order = jnp.arange(PER, dtype=jnp.int32)
    same = (owners[:, None] == owners[None, :]) & (order[None, :] < order[:, None])
    position = owners * 2 + jnp.sum(same.astype(jnp.int32), axis=1)
    hits = position.reshape(NBLK, NT)[:, :, None] == jnp.arange(SLOTS, dtype=jnp.int32)
    hits = hits.astype(BF)

    row = core * ROWS_C + z * SUB
    mine = lax.dynamic_slice_in_dim(features.reshape(NBLK, QB, width), row, SUB, axis=1)
    outgoing = jnp.einsum(
        "bs,bf->sf",
        hits.sum(axis=1),
        mine.reshape(NBLK, SUB * width),
        preferred_element_type=F32,
    ).astype(BF)
    arrived = lax.all_to_all(
        outgoing.reshape(TILES, 2 * SUB, width), ("x", "y"), 0, 0, tiled=True
    )

    memory = unitnorm_rows(features)
    queries = unitnorm_rows(arrived.reshape(SLOTS * SUB, width))
    scores = lax.dot_general(
        queries, memory, (((1,), (1,)), ((), ())), preferred_element_type=F32
    ) / SOFTMAX_TEMPER
    columns = jnp.arange(TILE, dtype=jnp.int32)
    scored = jnp.where(columns < valid_counts[0], jnp.exp(scores), 0.0).astype(BF)
    back = lax.all_to_all(
        scored.reshape(TILES, 2 * SUB, TILE), ("x", "y"), 0, 0, tiled=True
    ).reshape(SLOTS, SUB * TILE)
    chosen = jnp.einsum("bks,sf->bkf", hits, back, preferred_element_type=F32)
    chosen = chosen.reshape(NBLK, NT, SUB, TILE)
    denominator = jnp.sum(chosen, axis=(1, 3), keepdims=True)
    scaled = (ALPHA * chosen / denominator).astype(BF)
    scaled = scaled.transpose(0, 2, 1, 3).reshape(NBLK, SUB, NT * TILE)

    part = jnp.sum(jnp.exp(logits.astype(F32) + class_bias[None, :]), axis=1)
    high, middle, low = split_terms(part)
    terms = jnp.concatenate([high, middle, low, jnp.zeros_like(low)])
    piece = jnp.concatenate([scaled, terms.reshape(1, SUB, NT * TILE)])
    over_z = lax.all_to_all(
        jnp.broadcast_to(piece, (NZ,) + piece.shape), "z", 0, 0, tiled=True
    )

    piece = over_z[:, :NBLK].transpose(1, 0, 2, 3).reshape(NBLK * ROWS_C, NT * TILE)
    weights = lax.all_gather(piece, ("y", "c"), axis=0, tiled=False)

    terms = jnp.sum(over_z[:, NBLK].astype(F32), axis=0).reshape(4, rows)
    totals = terms[0] + terms[1] + terms[2]
    raw, _ = lax.optimization_barrier((logits, over_z))
    raw = lax.all_to_all(
        raw.T.reshape(NY, classes // NY, rows), "y", 0, 0, tiled=True
    )
    totals = totals + lax.ppermute(totals, "c", [(0, 1), (1, 0)])
    known = jnp.concatenate([totals, owners.astype(F32), jnp.zeros((128 - PER,), F32)])
    raw = around_x(raw)
    known, _ = lax.optimization_barrier((known, (raw[1], raw[4])))
    known = lax.all_to_all(
        jnp.broadcast_to(known, (TILES,) + known.shape), ("x", "y"), 0, 0, tiled=True
    )
    known = known.reshape(NX, NY, -1)
    known = lax.dynamic_slice_in_dim(jnp.concatenate([known, known]), x, NX, axis=0)
    totals = known[:, :, :rows]

    bias = lax.dynamic_slice_in_dim(class_bias.reshape(NY, classes // NY), y, 1, axis=0)
    bias = bias.reshape(1, classes // NY, 1)
    half = NY // 2
    sums = totals[0], totals[1], totals[2, :half], totals[2, half:], totals[3]
    priors = tuple(
        (jnp.exp(r.astype(F32) + bias) / t[:, None, :]).astype(BF) for r, t in zip(raw, sums)
    )

    named = known[0, :, rows : rows + PER].astype(jnp.int32).reshape(NY * PER)
    index = (named // NY - x) % NX * NY + named % NY

    labels = sweep(index, weights, priors[0], priors, 48)
    spread = sweep(index, weights, priors[0], around_x(labels), 16)
    spread = lax.all_to_all(spread, "y", 0, 0, tiled=True)
    return jnp.log(spread.reshape(classes, rows).T.astype(F32))


def solution(mesh):
    split = Mesh(mesh.devices.reshape(NX, NY, NZ, NC), ("x", "y", "z", "c"))
    dp, tensor = ("x", "y"), ("z", "c")
    in_specs = (P(dp, None), P(tensor), P(dp, tensor), P(dp, None), P(dp))
    return jax.shard_map(
        on_device, mesh=split, in_specs=in_specs, out_specs=P(dp, tensor), check_vma=False
    )
```

```python
import math

import jax
import jax.numpy as jnp
from jax import lax
from jax.experimental import pallas as pl
from jax.experimental.pallas import tpu as pltpu
from jax.sharding import Mesh
from jax.sharding import PartitionSpec as P

ALPHA = 0.75
SOFTMAX_TEMPER = 0.05
EPSILON = 1e-06

NX, NY, NZ, NC = 4, 8, 8, 2
TILES = NX * NY
TILE = 512
QB = 32
NBLK = 16
NT = 2
PER = NBLK * NT
SLOTS = TILES * 2
SUB = 2
ROWS_C = QB // NC
BF = jnp.bfloat16
F32 = jnp.float32


def unitnorm_rows(features):
    wide = features.astype(F32)
    scale = lax.rsqrt(jnp.mean(wide * wide, axis=-1, keepdims=True) + EPSILON)
    return (wide * scale / math.sqrt(wide.shape[-1])).astype(BF)


def sweep_kernel(index_ref, w_ref, prior_ref, own, after, oppa, oppb, before, out_ref, held, sems):
    y = pl.program_id(0)

    @pl.when(y == 0)
    def _():
        half = NY // 2
        places = (
            (own, 0, NY),
            (after, NY, NY),
            (oppa, 2 * NY, half),
            (oppb, 2 * NY + half, half),
            (before, 3 * NY, NY),
        )
        copies = [
            pltpu.make_async_copy(src, held.at[pl.ds(at, n)], sems.at[i])
            for i, (src, at, n) in enumerate(places)
        ]
        for copy in copies:
            copy.start()
        for copy in copies:
            copy.wait()

    classes = out_ref.shape[1]
    lanes = lax.broadcasted_iota(jnp.int32, (classes, 128), 1) // QB
    for group in range(NBLK // 4):
        total = None
        for k in range(NT):
            weights = jnp.concatenate(
                [
                    w_ref[c, pl.ds((4 * group + b) * ROWS_C, ROWS_C), pl.ds(k * TILE, TILE)]
                    for b in range(4)
                    for c in range(NC)
                ],
                axis=0,
            )
            labels = jnp.concatenate(
                [held[index_ref[y * PER + (4 * group + b) * NT + k]] for b in range(4)], axis=0
            )
            sums = lax.dot_general(
                labels, weights, (((1,), (1,)), ((), ())), preferred_element_type=F32
            )
            total = sums if total is None else total + sums
        picked = total[:classes]
        for b in range(1, 4):
            picked = jnp.where(lanes == b, total[b * classes : (b + 1) * classes], picked)
        at = pl.ds(128 * group, 128)
        prior = prior_ref[0, :, at].astype(F32)
        out_ref[0, :, at] = (picked + (1.0 - ALPHA) * prior).astype(BF)


def sweep(index, weights, prior, pieces, grant):
    ny, classes, rows = prior.shape
    return pl.pallas_call(
        sweep_kernel,
        grid_spec=pltpu.PrefetchScalarGridSpec(
            num_scalar_prefetch=1,
            grid=(ny,),
            in_specs=[
                pl.BlockSpec((NC,) + weights.shape[1:], lambda y, _: (y, 0, 0)),
                pl.BlockSpec((1, classes, rows), lambda y, _: (y, 0, 0)),
            ]
            + [pl.BlockSpec(memory_space=pl.ANY)] * len(pieces),
            out_specs=pl.BlockSpec((1, classes, rows), lambda y, _: (y, 0, 0)),
            scratch_shapes=[
                pltpu.VMEM((TILES, classes, rows), BF),
                pltpu.SemaphoreType.DMA((len(pieces),)),
            ],
        ),
        out_shape=jax.ShapeDtypeStruct(prior.shape, BF),
        compiler_params=pltpu.CompilerParams(vmem_limit_bytes=grant << 20),
        cost_estimate=pl.CostEstimate(
            flops=2 * ny * rows * NT * TILE * classes * 4,
            bytes_accessed=weights.size * 2 + 4 * prior.size * 2,
            transcendentals=0,
        ),
    )(index, weights, prior, *pieces)


def around_x(mine):
    forward = [(i, (i + 1) % NX) for i in range(NX)]
    backward = [(i, (i - 1) % NX) for i in range(NX)]
    before = lax.ppermute(mine, "x", forward)
    after = lax.ppermute(mine, "x", backward)
    half = NY // 2
    oppa = lax.ppermute(before[:half], "x", forward)
    oppb = lax.ppermute(after[half:], "x", backward)
    return mine, after, oppa, oppb, before


def split_terms(value):
    terms = []
    for scale in (0.99, 1.0, 1.0):
        term = (value * scale).astype(BF)
        value = value - term.astype(F32)
        terms.append(term)
    return terms


def on_device(features, class_bias, logits, tile_lists, valid_counts):
    width = features.shape[1]
    rows, classes = logits.shape
    x, y = lax.axis_index("x"), lax.axis_index("y")
    z, core = lax.axis_index("z"), lax.axis_index("c")

    lists = tile_lists.T
    order = jnp.arange(PER, dtype=jnp.int32).reshape(NT, NBLK)
    same = (lists[:, :, None, None] == lists) & (order[:, :, None, None] > order)
    position = lists * 2 + jnp.sum(same.astype(jnp.int32), axis=(2, 3))
    hits = position[:, :, None] == jnp.arange(SLOTS, dtype=jnp.int32)
    hits = hits.astype(BF)
    owners = tile_lists.reshape(PER)

    row = core * ROWS_C + z * SUB
    mine = lax.dynamic_slice_in_dim(features.reshape(NBLK, QB, width), row, SUB, axis=1)
    outgoing = jnp.einsum(
        "bs,bf->sf",
        hits.sum(axis=0),
        mine.reshape(NBLK, SUB * width),
        preferred_element_type=F32,
    ).astype(BF)
    arrived = lax.all_to_all(
        outgoing.reshape(TILES, 2 * SUB, width), ("x", "y"), 0, 0, tiled=True
    )

    memory = unitnorm_rows(features)
    queries = unitnorm_rows(arrived.reshape(SLOTS * SUB, width))
    scores = lax.dot_general(
        queries, memory, (((1,), (1,)), ((), ())), preferred_element_type=F32
    ) / SOFTMAX_TEMPER
    columns = jnp.arange(TILE, dtype=jnp.int32)
    scored = jnp.where(columns < valid_counts[0], jnp.exp(scores), 0.0).astype(BF)
    back = lax.all_to_all(
        scored.reshape(TILES, 2 * SUB, TILE), ("x", "y"), 0, 0, tiled=True
    ).reshape(SLOTS, SUB * TILE)
    chosen = jnp.einsum("kbs,sf->bkf", hits, back, preferred_element_type=F32)
    chosen = chosen.reshape(NBLK, NT, SUB, TILE)
    denominator = jnp.sum(chosen, axis=(1, 3), keepdims=True)
    scaled = (ALPHA * chosen / denominator).astype(BF)
    scaled = scaled.transpose(0, 2, 1, 3).reshape(NBLK, SUB, NT * TILE)

    part = jnp.sum(jnp.exp(logits.astype(F32) + class_bias[None, :]), axis=1)
    high, middle, low = split_terms(part)
    terms = jnp.concatenate([high, middle, low, jnp.zeros_like(low)])
    piece = jnp.concatenate([scaled, terms.reshape(1, SUB, NT * TILE)])
    over_z = lax.all_to_all(
        jnp.broadcast_to(piece, (NZ,) + piece.shape), "z", 0, 0, tiled=True
    )

    piece = over_z[:, :NBLK].transpose(1, 0, 2, 3).reshape(NBLK * ROWS_C, NT * TILE)
    weights = lax.all_gather(piece, ("y", "c"), axis=0, tiled=False)

    terms = jnp.sum(over_z[:, NBLK].astype(F32), axis=0).reshape(4, rows)
    totals = terms[0] + terms[1] + terms[2]
    raw, _ = lax.optimization_barrier((logits, over_z))
    raw = lax.all_to_all(
        raw.T.reshape(NY, classes // NY, rows), "y", 0, 0, tiled=True
    )
    totals = totals + lax.ppermute(totals, "c", [(0, 1), (1, 0)])
    known = jnp.concatenate([totals, owners.astype(F32), jnp.zeros((128 - PER,), F32)])
    known, _ = lax.optimization_barrier((known, raw))
    known = lax.all_to_all(
        jnp.broadcast_to(known, (TILES,) + known.shape), ("x", "y"), 0, 0, tiled=True
    )
    raw = around_x(raw)
    known = known.reshape(NX, NY, -1)
    known = lax.dynamic_slice_in_dim(jnp.concatenate([known, known]), x, NX, axis=0)
    totals = known[:, :, :rows]

    bias = lax.dynamic_slice_in_dim(class_bias.reshape(NY, classes // NY), y, 1, axis=0)
    bias = bias.reshape(1, classes // NY, 1)
    half = NY // 2
    sums = totals[0], totals[1], totals[2, :half], totals[2, half:], totals[3]
    priors = tuple(
        (jnp.exp(r.astype(F32) + bias) / t[:, None, :]).astype(BF) for r, t in zip(raw, sums)
    )

    named = known[0, :, rows : rows + PER].astype(jnp.int32).reshape(NY * PER)
    index = (named // NY - x) % NX * NY + named % NY

    labels = sweep(index, weights, priors[0], priors, 48)
    spread = sweep(index, weights, priors[0], around_x(labels), 16)
    spread = lax.all_to_all(spread, "y", 0, 0, tiled=True)
    return jnp.log(spread.reshape(classes, rows).T.astype(F32))


def solution(mesh):
    split = Mesh(mesh.devices.reshape(NX, NY, NZ, NC), ("x", "y", "z", "c"))
    dp, tensor = ("x", "y"), ("z", "c")
    in_specs = (P(dp, None), P(tensor), P(dp, tensor), P(dp, None), P(dp))
    return jax.shard_map(
        on_device, mesh=split, in_specs=in_specs, out_specs=P(dp, tensor), check_vma=False
    )
```
